32 devices in a mesh: hel: 4 (over y, core), rad: 8 (over z, x).
Axes of the slice: x: 2, y: 2, z: 4, core: 2. Of those that a mesh axis runs over, the one named last changes fastest.
Arguments:
- older_packet: float32 [4, 512, 8, 1024], P('hel', 'rad'), may hold values from -6 to 6
- newer_packet: float32 [4, 512, 8, 1024], P('hel', 'rad'), may hold values from -6 to 6
- kinetic: bfloat16 [512, 512], replicated, may hold values from -1 to 1, as said below
- transform: bfloat16 [4, 1024, 1024], P('hel'), may hold values from -0.1875 to 0.1875
- potential: bfloat16 [512, 8, 1024], P('rad'), may hold values from -2 to 2
- coupling: bfloat16 [4, 1024], P('hel'), may hold values from 0.29882812 to 1.5
- radial_weight: float32 [512], replicated, may hold values from 0.3 to 2
- damping: float32 [512], P('rad'), may hold values from 0.6 to 1
Outputs:
- older_out: float32 [4, 512, 8, 1024], P('hel', 'rad')
- newer_out: float32 [4, 512, 8, 1024], P('hel', 'rad')
The draws below stay inside these ranges and needn't reach their ends.
Inputs may be any that keep to these rules, and one draw needn't show every extreme that they name: kinetic is symmetric.
All inputs are finite; a program needn't handle non-finite values.
Results may differ from the reference program's by a relative error of at most 0.014.
Values may be sent and summed in bfloat16 or wider, within the bound.
A program may use at most 64 MiB of HBM per device.

```python
import math
import jax
import jax.numpy as jnp
from jax import lax

RADIAL = 512
VIBRATION = 8
ANGULAR = 1024
STEPS = 3
HELICITY = 4


def draw_kinetic(key, part):
    first = jax.random.fold_in(jax.random.fold_in(key, 17), 0)
    noise = jax.random.truncated_normal(first, -4.0, 4.0, (RADIAL, RADIAL), jnp.float32)
    sym = (noise + noise.T) * (0.5 / RADIAL ** 0.5)
    return jnp.clip(sym, -1.0, 1.0).astype(jnp.bfloat16)


def steps_of(own_key, dims, cuts, low, high):
    loudness = 1.0
    for axis_at, blocks in cuts:
        draws = jax.random.uniform(jax.random.fold_in(jax.random.fold_in(own_key, 6), axis_at), (blocks,), jnp.float32, low / len(cuts), high / len(cuts))
        loudness = loudness * jnp.repeat(jnp.exp(draws), dims[axis_at] // blocks).reshape((-1,) + (1,) * (len(dims) - 1 - axis_at))
    return loudness


def bell_draw(key, extent, width, reach, cuts=(), held_as=jnp.bfloat16):
    values = width * jax.random.normal(key, extent, jnp.float32)
    if cuts:
        values = values * steps_of(key, extent, cuts, -0.22, 0.18)
    return jnp.clip(values, -reach, reach).astype(held_as)


def setup_inputs(seed: int = 0) -> dict:
    streams_of = jax.random.split(jax.random.key(seed), 9)
    older_packet = bell_draw(streams_of[0], (HELICITY, RADIAL, VIBRATION, ANGULAR), 1.0, 6.0, ((0, 4), (1, 8)), jnp.float32)
    newer_packet = bell_draw(streams_of[1], (HELICITY, RADIAL, VIBRATION, ANGULAR), 1.0, 6.0, ((0, 4), (1, 8)), jnp.float32)
    kinetic = draw_kinetic(jax.random.fold_in(streams_of[8], 71), 0)
    transform = bell_draw(streams_of[3], (HELICITY, ANGULAR, ANGULAR), ANGULAR ** -0.5, 0.1875, ((0, 4),))
    potential = jnp.clip(jax.random.uniform(streams_of[4], (RADIAL, VIBRATION, ANGULAR), jnp.float32, -2.0, 2.0) * steps_of(streams_of[4], (RADIAL, VIBRATION, ANGULAR), ((0, 8),), -0.4, 0.0), -2.0, 2.0).astype(jnp.bfloat16)
    coupling = jnp.clip(jnp.exp(math.log(1.5) - 1.6133518 * jax.random.uniform(streams_of[5], (HELICITY, ANGULAR), jnp.float32) ** steps_of(streams_of[5], (HELICITY, ANGULAR), ((0, 4),), -0.2, 0.2)), 0.29882812, 1.5).astype(jnp.bfloat16)
    radial_weight = jnp.clip(jnp.exp(jax.random.uniform(streams_of[6], (RADIAL,), jnp.float32, math.log(0.3), math.log(2.0))), 0.3, 2.0)
    damping = jnp.clip(0.6 + 0.39999998 * jax.random.uniform(streams_of[7], (RADIAL,), jnp.float32) ** steps_of(streams_of[7], (RADIAL,), ((0, 8),), -0.2, 0.2), 0.6, 1.0)
    return {"older_packet": older_packet, "newer_packet": newer_packet, "kinetic": kinetic, "transform": transform, "potential": potential, "coupling": coupling, "radial_weight": radial_weight, "damping": damping}


SCALE_FACTOR = 0.35


def angular_block(rounded_block, matrix, potential_flat):
    flat = rounded_block.reshape(RADIAL * VIBRATION, ANGULAR)
    grid = jnp.dot(flat, matrix, preferred_element_type=jnp.float32)
    grid_values = (grid * potential_flat).astype(jnp.bfloat16)
    back = lax.dot_general(grid_values, matrix, (((1,), (1,)), ((), ())), preferred_element_type=jnp.float32)
    return back.reshape(RADIAL, VIBRATION, ANGULAR)


def reference(older_packet, newer_packet, kinetic, transform, potential, coupling, radial_weight, damping):
    kinetic_wide = kinetic.astype(jnp.float32)
    potential_flat = potential.astype(jnp.float32).reshape(RADIAL * VIBRATION, ANGULAR)
    coefficient = coupling.astype(jnp.float32)
    lower_coef = jnp.concatenate([jnp.zeros((1, ANGULAR), jnp.float32), coefficient[:-1]], axis=0)
    damp = damping[None, :, None, None]
    previous = older_packet
    current = newer_packet
    for _ in range(STEPS):
        rounded = current.astype(jnp.bfloat16)
        widened = rounded.astype(jnp.float32)
        radial_part = jnp.einsum("rs,ksva->krva", kinetic_wide, widened)
        empty = jnp.zeros((1, RADIAL, VIBRATION, ANGULAR), jnp.float32)
        below = jnp.concatenate([empty, widened[:-1]], axis=0)
        above = jnp.concatenate([widened[1:], empty], axis=0)
        coriolis_part = radial_weight[None, :, None, None] * (lower_coef[:, None, None, :] * below + coefficient[:, None, None, :] * above)
        off_grid = (radial_part + coriolis_part).astype(jnp.bfloat16)
        off_grid = lax.optimization_barrier(off_grid).astype(jnp.float32)
        angular_part = lax.map(lambda pair: angular_block(pair[0], pair[1], potential_flat), (rounded, transform))
        applied = SCALE_FACTOR * (off_grid + angular_part)
        following = damp * (2.0 * applied - damp * previous)
        previous = current
        current = following
    return previous, current
```

```python
import jax
import jax.numpy as jnp
from jax import lax
from jax.sharding import PartitionSpec as P

STEPS = 3


SCALE_FACTOR = 0.35


def from_behind(array, axis, by):
    devices = lax.axis_size(axis)
    pairs = [(i, i + by) for i in range(devices) if 0 <= i + by < devices]
    return lax.ppermute(array, axis, pairs)


def coriolis_term(block, coefs, weights):
    lower_block, lower_coefs = from_behind((block, coefs), "hel", 1)
    upper_block = from_behind(block, "hel", -1)
    below = jnp.concatenate([lower_block, block[:-1]], axis=0).astype(jnp.float32)
    below_coefs = jnp.concatenate([lower_coefs, coefs[:-1]], axis=0).astype(jnp.float32)
    above = jnp.concatenate([block[1:], upper_block], axis=0).astype(jnp.float32)
    mixed = below_coefs[:, None, :] * below + coefs.astype(jnp.float32)[:, None, :] * above
    return weights[None, :, None] * mixed


def body(
    older_packet, newer_packet, kinetic, transform, potential, coupling, radial_weight, damping
):
    hel_rows, rad_rows, vib_count, ang_count = newer_packet.shape
    flat_width = vib_count * ang_count
    rank = lax.axis_index("rad")
    previous = older_packet.reshape(hel_rows, rad_rows, flat_width)
    current = newer_packet.reshape(hel_rows, rad_rows, flat_width)
    potential_flat = potential.astype(jnp.float32).reshape(1, rad_rows * vib_count, ang_count)
    tiled_coefs = jnp.tile(coupling, (1, vib_count))
    damp = damping[None, :, None]
    for _ in range(STEPS):
        rounded = current.astype(jnp.bfloat16)
        regrouped = lax.all_to_all(rounded, "rad", split_axis=2, concat_axis=1, tiled=True)
        kinetic_term = jnp.einsum(
            "rs,ksc->krc", kinetic, regrouped, preferred_element_type=jnp.float32
        )
        returned = lax.all_to_all(kinetic_term, "rad", split_axis=1, concat_axis=2, tiled=True)
        start = rank * rad_rows
        local_weights = lax.dynamic_slice_in_dim(radial_weight, start, rad_rows, 0)
        summed = returned + coriolis_term(rounded, tiled_coefs, local_weights)
        off_grid = summed.astype(jnp.bfloat16).astype(jnp.float32)
        angular_rows = rounded.reshape(hel_rows, rad_rows * vib_count, ang_count)
        grid = jnp.einsum(
            "kna,kag->kng", angular_rows, transform, preferred_element_type=jnp.float32
        )
        grid_values = (grid * potential_flat).astype(jnp.bfloat16)
        angular_part = jnp.einsum(
            "kng,kag->kna", grid_values, transform, preferred_element_type=jnp.float32
        )
        applied = SCALE_FACTOR * (off_grid + angular_part.reshape(hel_rows, rad_rows, flat_width))
        following = damp * (2.0 * applied - damp * previous)
        previous = current
        current = following
    shape = (hel_rows, rad_rows, vib_count, ang_count)
    return (previous.reshape(shape), current.reshape(shape))


def by_vibration(
    older_packet, newer_packet, kinetic, transform, potential, coupling, radial_weight, damping
):
    hel_rows, rad_rows, vib_count, ang_count = newer_packet.shape
    devices = lax.axis_size("rad")

    def scatter(array):
        return lax.all_to_all(array, "rad", split_axis=2, concat_axis=1, tiled=True)

    rounded = scatter(newer_packet.astype(jnp.bfloat16))
    previous = scatter(older_packet.astype(jnp.bfloat16)).astype(jnp.float32)
    pot = scatter(potential[None])[0].astype(jnp.float32)
    damp = lax.all_gather(damping, "rad", tiled=True)[None, :, None, None]
    weight = radial_weight[None, :, None, None]
    current = rounded.astype(jnp.float32)
    lower_coefs = from_behind(coupling, "hel", 1)
    coefs = jnp.concatenate([lower_coefs, coupling], axis=0).astype(jnp.float32)
    coefs = coefs[:, None, None, :]
    history = []
    for step in range(STEPS):
        lower = from_behind(rounded[-1:], "hel", 1)
        upper = from_behind(rounded[:1], "hel", -1)
        padded = jnp.concatenate([lower, rounded, upper], axis=0).astype(jnp.float32)
        mixed = coefs[:-1] * padded[:-2] + coefs[1:] * padded[2:]
        radial = jnp.einsum(
            "rs,ksva->krva", kinetic, rounded, preferred_element_type=jnp.float32
        )
        off_grid = radial + weight * mixed
        grid = jnp.einsum(
            "krva,kag->krvg", rounded, transform, preferred_element_type=jnp.float32
        )
        grid_values = (grid * pot[None]).astype(jnp.bfloat16)
        angular = jnp.einsum(
            "krvg,kag->krva", grid_values, transform, preferred_element_type=jnp.float32
        )
        applied = SCALE_FACTOR * (off_grid + angular)
        following = damp * (2.0 * applied - damp * previous)
        previous = current
        current = following
        rounded = current.astype(jnp.bfloat16)
        history.append(rounded)

    def gather(array):
        back = lax.all_to_all(array, "rad", split_axis=1, concat_axis=2, tiled=True)
        return back.astype(jnp.float32)

    return gather(history[-2]), gather(history[-1])


def whole_body(older_packet, newer_packet, *rest):
    if newer_packet.shape[2] % lax.axis_size("rad") == 0:
        return by_vibration(older_packet, newer_packet, *rest)
    return body(older_packet, newer_packet, *rest)


def solution(mesh):
    return jax.shard_map(
        whole_body,
        mesh=mesh,
        in_specs=(
            P("hel", "rad", None, None),
            P("hel", "rad", None, None),
            P(),
            P("hel", None, None),
            P("rad", None, None),
            P("hel", None),
            P(),
            P("rad"),
        ),
        out_specs=(P("hel", "rad", None, None), P("hel", "rad", None, None)),
        check_vma=False,
    )
```

```python
import functools

import jax
import jax.numpy as jnp
from jax import lax
from jax.experimental import pallas as pl
from jax.experimental.pallas import tpu as pltpu
from jax.sharding import PartitionSpec as P

STEPS = 3


SCALE_FACTOR = 0.35


def from_behind(array, axis, by):
    devices = lax.axis_size(axis)
    pairs = [(i, i + by) for i in range(devices) if 0 <= i + by < devices]
    return lax.ppermute(array, axis, pairs)


def coriolis_term(block, coefs, weights):
    lower_block, lower_coefs = from_behind((block, coefs), "hel", 1)
    upper_block = from_behind(block, "hel", -1)
    below = jnp.concatenate([lower_block, block[:-1]], axis=0).astype(jnp.float32)
    below_coefs = jnp.concatenate([lower_coefs, coefs[:-1]], axis=0).astype(jnp.float32)
    above = jnp.concatenate([block[1:], upper_block], axis=0).astype(jnp.float32)
    mixed = below_coefs[:, None, :] * below + coefs.astype(jnp.float32)[:, None, :] * above
    return weights[None, :, None] * mixed


def body(
    older_packet, newer_packet, kinetic, transform, potential, coupling, radial_weight, damping
):
    hel_rows, rad_rows, vib_count, ang_count = newer_packet.shape
    flat_width = vib_count * ang_count
    rank = lax.axis_index("rad")
    previous = older_packet.reshape(hel_rows, rad_rows, flat_width)
    current = newer_packet.reshape(hel_rows, rad_rows, flat_width)
    potential_flat = potential.astype(jnp.float32).reshape(1, rad_rows * vib_count, ang_count)
    tiled_coefs = jnp.tile(coupling, (1, vib_count))
    damp = damping[None, :, None]
    for _ in range(STEPS):
        rounded = current.astype(jnp.bfloat16)
        regrouped = lax.all_to_all(rounded, "rad", split_axis=2, concat_axis=1, tiled=True)
        kinetic_term = jnp.einsum(
            "rs,ksc->krc", kinetic, regrouped, preferred_element_type=jnp.float32
        )
        returned = lax.all_to_all(kinetic_term, "rad", split_axis=1, concat_axis=2, tiled=True)
        start = rank * rad_rows
        local_weights = lax.dynamic_slice_in_dim(radial_weight, start, rad_rows, 0)
        summed = returned + coriolis_term(rounded, tiled_coefs, local_weights)
        off_grid = summed.astype(jnp.bfloat16).astype(jnp.float32)
        angular_rows = rounded.reshape(hel_rows, rad_rows * vib_count, ang_count)
        grid = jnp.einsum(
            "kna,kag->kng", angular_rows, transform, preferred_element_type=jnp.float32
        )
        grid_values = (grid * potential_flat).astype(jnp.bfloat16)
        angular_part = jnp.einsum(
            "kng,kag->kna", grid_values, transform, preferred_element_type=jnp.float32
        )
        applied = SCALE_FACTOR * (off_grid + angular_part.reshape(hel_rows, rad_rows, flat_width))
        following = damp * (2.0 * applied - damp * previous)
        previous = current
        current = following
    shape = (hel_rows, rad_rows, vib_count, ang_count)
    return (previous.reshape(shape), current.reshape(shape))


def by_vibration(
    older_packet, newer_packet, kinetic, transform, potential, coupling, radial_weight, damping
):
    hel_rows, rad_rows, vib_count, ang_count = newer_packet.shape
    devices = lax.axis_size("rad")

    def scatter(array):
        return lax.all_to_all(array, "rad", split_axis=2, concat_axis=1, tiled=True)

    rounded = scatter(newer_packet.astype(jnp.bfloat16))
    previous = scatter(older_packet.astype(jnp.bfloat16)).astype(jnp.float32)
    pot = scatter(potential[None])[0].astype(jnp.float32)
    damp = lax.all_gather(damping, "rad", tiled=True)[None, :, None, None]
    weight = radial_weight[None, :, None, None]
    current = rounded.astype(jnp.float32)
    lower_coefs = from_behind(coupling, "hel", 1)
    coefs = jnp.concatenate([lower_coefs, coupling], axis=0).astype(jnp.float32)
    coefs = coefs[:, None, None, :]
    history = []
    for step in range(STEPS):
        lower = from_behind(rounded[-1:], "hel", 1)
        upper = from_behind(rounded[:1], "hel", -1)
        padded = jnp.concatenate([lower, rounded, upper], axis=0).astype(jnp.float32)
        mixed = coefs[:-1] * padded[:-2] + coefs[1:] * padded[2:]
        radial = jnp.einsum(
            "rs,ksva->krva", kinetic, rounded, preferred_element_type=jnp.float32
        )
        off_grid = radial + weight * mixed
        grid = jnp.einsum(
            "krva,kag->krvg", rounded, transform, preferred_element_type=jnp.float32
        )
        grid_values = (grid * pot[None]).astype(jnp.bfloat16)
        angular = jnp.einsum(
            "krvg,kag->krva", grid_values, transform, preferred_element_type=jnp.float32
        )
        applied = SCALE_FACTOR * (off_grid + angular)
        following = damp * (2.0 * applied - damp * previous)
        previous = current
        current = following
        rounded = current.astype(jnp.bfloat16)
        history.append(rounded)

    def gather(array):
        back = lax.all_to_all(array, "rad", split_axis=1, concat_axis=2, tiled=True)
        return back.astype(jnp.float32)

    return gather(history[-2]), gather(history[-1])


MESH = pl.DeviceIdType.MESH
POT, NEW, OLD, DAMP, OUT3, OUT4 = range(6)


def packet_kernel(
    n, hels,
    newer, older, kinetic, transform, potential, coupling, weight, damping,
    out_old, out_new,
    newer_v, older_v, kin, tr, pot_in, pot_wide, coef, coef_low, damp_own, damp_all, weight_all,
    damp_col, weight_col, send_pot, send_new, send_old, pot, x0, x1, x2, x3, x4, total, grid,
    low, high, back3, back4,
    in_sem, lane_sem, out_sem, rad_send, rad_recv, pot_send, pot_recv, hel_send, hel_recv, coef_sem,
):
    me = lax.axis_index("rad")
    hel = lax.axis_index("hel")
    rows = send_new.shape[1]
    ang = newer.shape[1]
    width = ang // hels
    has_low = hel > 0
    has_high = hel < hels - 1

    def shift(i):
        if n % 2:
            return i + 1
        return n // 2 + ((i + 1) // 2) * (1 - 2 * (i % 2))

    def target(i):
        return lax.rem(me + shift(i), n)

    def source(i):
        return lax.rem(me - shift(i) + n, n)

    def block(c):
        return pl.ds(pl.multiple_of(c * rows, rows), rows)

    loads = [
        pltpu.make_async_copy(src, dst, in_sem.at[s])
        for s, (src, dst) in enumerate(
            (
                (potential.at[:, :, pl.ds(pl.multiple_of(hel * width, width), width)], pot_in),
                (damping, damp_own),
                (coupling, coef),
                (weight, weight_all),
                (kinetic, kin),
                (transform, tr),
            )
        )
    ]

    def lanes(l):
        return pl.ds(pl.multiple_of(l * 128, 128), 128)

    def newer_load(l):
        return pltpu.make_async_copy(newer.at[:, lanes(l)], newer_v.at[l], lane_sem.at[0, l])

    def older_load(l):
        return pltpu.make_async_copy(older.at[:, lanes(l)], older_v.at[l], lane_sem.at[1, l])

    def each_lane(copy, method):
        @pl.loop(0, ang // 128)
        def _(l):
            getattr(copy(l), method)()

    for load in loads[:3]:
        load.start()
    each_lane(newer_load, "start")
    each_lane(older_load, "start")
    for load in loads[3:]:
        load.start()

    barrier = pltpu.get_barrier_semaphore()

    @pl.loop(1, n)
    def _(j):
        pl.semaphore_signal(
            barrier, inc=1, device_id={"rad": lax.rem(me + j, n)}, device_id_type=MESH
        )

    @pl.loop(1, hels)
    def _(j):
        pl.semaphore_signal(
            barrier, inc=1, device_id={"hel": lax.rem(hel + j, hels)}, device_id_type=MESH
        )

    pl.semaphore_wait(barrier, n + hels - 2)

    def over_rad(kind, src, dst, i):
        return pltpu.make_async_remote_copy(
            src_ref=src,
            dst_ref=dst,
            send_sem=rad_send.at[kind, i],
            recv_sem=rad_recv.at[kind, i],
            device_id={"rad": target(i)},
            device_id_type=MESH,
        )

    def pot_copy(i):
        return over_rad(POT, send_pot.at[i], pot.at[hel, block(me)], i)

    def new_copy(i):
        return over_rad(NEW, send_new.at[i], x1.at[block(me)], i)

    def old_copy(i):
        return over_rad(OLD, send_old.at[i], x0.at[block(me)], i)

    def damp_copy(i):
        return over_rad(DAMP, damp_own, damp_all.at[me], i)

    def out3_copy(i):
        return over_rad(OUT3, x3.at[block(target(i))], back3.at[me], i)

    def out4_copy(i):
        return over_rad(OUT4, x4.at[block(target(i))], back4.at[me], i)

    def pot_share(j):
        return pltpu.make_async_remote_copy(
            src_ref=pot.at[hel],
            dst_ref=pot.at[hel],
            send_sem=pot_send.at[j],
            recv_sem=pot_recv.at[j],
            device_id={"hel": lax.rem(hel + j, hels)},
            device_id_type=MESH,
        )

    coef_copy = pltpu.make_async_remote_copy(
        src_ref=coef,
        dst_ref=coef_low,
        send_sem=coef_sem.at[0],
        recv_sem=coef_sem.at[1],
        device_id={"hel": lax.rem(hel + 1, hels)},
        device_id_type=MESH,
    )

    def hel_up(step, x, c, sem):
        return pltpu.make_async_remote_copy(
            src_ref=x.at[c],
            dst_ref=low.at[step, c],
            send_sem=hel_send.at[step, 0, sem],
            recv_sem=hel_recv.at[step, 0, sem],
            device_id={"hel": lax.rem(hel + 1, hels)},
            device_id_type=MESH,
        )

    def hel_down(step, x, c, sem):
        return pltpu.make_async_remote_copy(
            src_ref=x.at[c],
            dst_ref=high.at[step, c],
            send_sem=hel_send.at[step, 1, sem],
            recv_sem=hel_recv.at[step, 1, sem],
            device_id={"hel": lax.rem(hel - 1 + hels, hels)},
            device_id_type=MESH,
        )

    def hel_start(step, x, c, sem):
        @pl.when(has_high)
        def _():
            hel_up(step, x, c, sem).start()

        @pl.when(has_low)
        def _():
            hel_down(step, x, c, sem).start()

    def hel_wait_recv(step, x, c, sem):
        @pl.when(has_low)
        def _():
            hel_up(step, x, c, sem).wait_recv()

        @pl.when(has_high)
        def _():
            hel_down(step, x, c, sem).wait_recv()

    def hel_wait_send(step, x, c, sem):
        @pl.when(has_high)
        def _():
            hel_up(step, x, c, sem).wait_send()

        @pl.when(has_low)
        def _():
            hel_down(step, x, c, sem).wait_send()

    def trailing(make, copy):
        @pl.loop(0, n - 1)
        def _(i):
            make(i)

            @pl.when(i > 0)
            def _():
                copy(i - 1).start()

    everything = pl.ds(0, n * rows)

    loads[0].wait()
    for l in range(width // 128):
        part = pot_in[:, :, 128 * l : 128 * (l + 1)].astype(jnp.float32)
        pot_wide[l] = part.reshape(pot_wide.shape[1:])

    def picked(ref, c):
        return jnp.concatenate(
            [
                ref[l, pl.ds(c, rows, stride=n), :]
                for l in range(ref.shape[0])
            ],
            axis=1,
        ).astype(jnp.bfloat16)

    def make_pot(i):
        send_pot[i] = picked(pot_wide, target(i))

    trailing(make_pot, pot_copy)
    pot[hel, block(me)] = picked(pot_wide, me)
    pot_copy(n - 2).start()

    each_lane(newer_load, "wait")

    def make_new(i):
        send_new[i] = picked(newer_v, target(i))

    trailing(make_new, new_copy)
    x1[block(me)] = picked(newer_v, me)
    new_copy(n - 2).start()

    loads[1].wait()
    loads[2].wait()

    @pl.loop(0, n - 1)
    def _(i):
        damp_copy(i).start()

    @pl.when(has_high)
    def _():
        coef_copy.start()

    each_lane(older_load, "wait")

    def make_old(i):
        send_old[i] = picked(older_v, target(i))

    trailing(make_old, old_copy)
    x0[block(me)] = picked(older_v, me)
    old_copy(n - 2).start()
    damp_all[me] = damp_own[...]

    @pl.when(jnp.logical_not(has_low))
    def _():
        low[...] = jnp.zeros_like(low)
        coef_low[...] = jnp.zeros_like(coef_low)

    @pl.when(jnp.logical_not(has_high))
    def _():
        high[...] = jnp.zeros_like(high)

    for load in loads[3:]:
        load.wait()

    @pl.loop(0, n - 1)
    def _(i):
        pot_copy(i).wait_recv()

    @pl.loop(1, hels)
    def _(j):
        pot_share(j).start()

    @pl.loop(0, n - 1)
    def _(i):
        damp_copy(i).wait_recv()

    @pl.when(has_low)
    def _():
        coef_copy.wait_recv()

    line = lax.broadcasted_iota(jnp.int32, (rows, rows), 0)
    lane = lax.broadcasted_iota(jnp.int32, (rows, rows), 1)

    def column(row):
        diagonal = jnp.where(line == lane, jnp.broadcast_to(row, (rows, rows)), 0.0)
        return jnp.broadcast_to(jnp.sum(diagonal, axis=1, keepdims=True), (rows, 128))

    @pl.loop(0, n)
    def _(c):
        damp_col[block(c)] = column(damp_all[c])
        weight_col[block(c)] = column(weight_all[c])

    @pl.loop(0, n - 1)
    def _(i):
        new_copy(i).wait_recv()

    hel_start(0, x1, everything, 0)

    @pl.loop(1, hels)
    def _(j):
        pot_share(j).wait_recv()

    def tile(t):
        return pl.ds(pl.multiple_of(t * width, width), width)

    def multiply(x):
        @pl.loop(0, hels)
        def _(t):
            values = jnp.dot(x[...], tr[:, tile(t)], preferred_element_type=jnp.float32)
            grid[:, tile(t)] = (values * pot[t].astype(jnp.float32)).astype(jnp.bfloat16)

        @pl.loop(0, hels)
        def _(t):
            radial = jnp.dot(kin[...], x[:, tile(t)], preferred_element_type=jnp.float32)
            angular = lax.dot_general(
                grid[...],
                tr[tile(t), :],
                (((1,), (1,)), ((), ())),
                preferred_element_type=jnp.float32,
            )
            total[:, tile(t)] = radial + angular

    lower_coef = coef_low[...].astype(jnp.float32)
    upper_coef = coef[...].astype(jnp.float32)

    def finish(step, prev, c):
        span = block(c)
        damp = damp_col[span, 0:1]
        mixed = lower_coef * low[step, span].astype(jnp.float32)
        mixed = mixed + upper_coef * high[step, span].astype(jnp.float32)
        applied = SCALE_FACTOR * (total[span] + weight_col[span, 0:1] * mixed)
        following = damp * (2.0 * applied - damp * prev[span].astype(jnp.float32))
        return following.astype(jnp.bfloat16)

    multiply(x1)
    hel_wait_recv(0, x1, everything, 0)
    x2[block(me)] = finish(0, x0, me)

    @pl.loop(0, n - 1)
    def _(i):
        old_copy(i).wait_recv()
        x2[block(source(i))] = finish(0, x0, source(i))

        @pl.when(i == 0)
        def _():
            hel_start(1, x2, block(me), 0)

        @pl.when(i > 0)
        def _():
            hel_start(1, x2, block(source(i - 1)), n - shift(i - 1))

    hel_start(1, x2, block(source(n - 2)), n - shift(n - 2))

    multiply(x2)

    @pl.loop(0, n)
    def _(i):
        hel_wait_recv(1, x2, block(lax.rem(me + i, n)), i)

    def make_out3(i):
        x3[block(target(i))] = finish(1, x1, target(i))

    trailing(make_out3, out3_copy)
    mine = finish(1, x1, me)
    x3[block(me)] = mine
    back3[me] = mine
    out3_copy(n - 2).start()
    hel_start(2, x3, everything, 0)

    multiply(x3)
    hel_wait_recv(2, x3, everything, 0)

    def make_out4(i):
        x4[block(target(i))] = finish(2, x2, target(i))

    trailing(make_out4, out4_copy)
    mine = finish(2, x2, me)
    x4[block(me)] = mine
    back4[me] = mine
    out4_copy(n - 2).start()

    def placed(ref, c, values):
        for l in range(ang // 128):
            ref[l, pl.ds(c, rows, stride=n), :] = values[
                :, 128 * l : 128 * (l + 1)
            ].astype(jnp.float32)

    def unload(wide, out, s, l):
        return pltpu.make_async_copy(wide.at[l], out.at[:, lanes(l)], out_sem.at[s, l])

    for copy, back, wide, out, s in (
        (out3_copy, back3, newer_v, out_old, 0),
        (out4_copy, back4, older_v, out_new, 1),
    ):
        placed(wide, me, back[me])

        @pl.loop(0, n - 1)
        def _(i):
            copy(i).wait_recv()
            placed(wide, source(i), back[source(i)])

        each_lane(functools.partial(unload, wide, out, s), "start")

    @pl.loop(0, n - 1)
    def _(i):
        for copy in (pot_copy, new_copy, old_copy, damp_copy, out3_copy, out4_copy):
            copy(i).wait_send()

    @pl.loop(1, hels)
    def _(j):
        pot_share(j).wait_send()

    @pl.when(has_high)
    def _():
        coef_copy.wait_send()

    hel_wait_send(0, x1, everything, 0)
    hel_wait_send(2, x3, everything, 0)

    @pl.loop(0, n)
    def _(i):
        hel_wait_send(1, x2, block(lax.rem(me + i, n)), i)

    each_lane(functools.partial(unload, newer_v, out_old, 0), "wait")
    each_lane(functools.partial(unload, older_v, out_new, 1), "wait")


def one_vibration(
    older_packet, newer_packet, kinetic, transform, potential, coupling, radial_weight, damping
):
    _, rows, n, ang = newer_packet.shape
    hels = lax.axis_size("hel")
    width = ang // hels
    points = n * rows
    bf16, f32 = jnp.bfloat16, jnp.float32
    vector = pltpu.VMEM((points, ang), bf16)
    blocks = pltpu.VMEM((n, rows, ang), bf16)
    wide = pltpu.VMEM((points, ang), f32)
    flat = jax.ShapeDtypeStruct((points, ang), f32)
    anywhere = pl.BlockSpec(memory_space=pl.ANY)
    sem = pltpu.SemaphoreType.DMA
    outs = pl.pallas_call(
        functools.partial(packet_kernel, n, hels),
        out_shape=(flat, flat),
        in_specs=[anywhere] * 8,
        out_specs=(anywhere, anywhere),
        scratch_shapes=[
            pltpu.VMEM((ang // 128, points, 128), f32),
            pltpu.VMEM((ang // 128, points, 128), f32),
            pltpu.VMEM((points, points), bf16),
            pltpu.VMEM((ang, ang), bf16),
            pltpu.VMEM((rows, n, width), bf16),
            pltpu.VMEM((width // 128, points, 128), f32),
            pltpu.VMEM((1, ang), bf16),
            pltpu.VMEM((1, ang), bf16),
            pltpu.VMEM((1, rows), f32),
            pltpu.VMEM((n, 1, rows), f32),
            pltpu.VMEM((n, 1, rows), f32),
            pltpu.VMEM((points, 128), f32),
            pltpu.VMEM((points, 128), f32),
            pltpu.VMEM((n, rows, width), bf16),
            blocks,
            blocks,
            pltpu.VMEM((hels, points, width), bf16),
            vector,
            vector,
            vector,
            vector,
            vector,
            wide,
            vector,
            pltpu.VMEM((STEPS, points, ang), bf16),
            pltpu.VMEM((STEPS, points, ang), bf16),
            blocks,
            blocks,
            sem((6,)),
            sem((2, ang // 128)),
            sem((2, ang // 128)),
            sem((6, n)),
            sem((6, n)),
            sem((hels,)),
            sem((hels,)),
            sem((STEPS, 2, n)),
            sem((STEPS, 2, n)),
            sem((2,)),
        ],
        compiler_params=pltpu.CompilerParams(
            collective_id=0, has_side_effects=True, vmem_limit_bytes=60 * 1024 * 1024
        ),
    )(
        newer_packet.reshape(points, ang),
        older_packet.reshape(points, ang),
        kinetic,
        transform[0],
        potential,
        coupling,
        radial_weight.reshape(n, 1, rows),
        damping.reshape(1, rows),
    )
    shape = newer_packet.shape
    return outs[0].reshape(shape), outs[1].reshape(shape)


def fits(packet):
    hel_rows, rows, vibs, ang = packet.shape
    hels = lax.axis_size("hel")
    return (
        STEPS == 3
        and hel_rows == 1
        and vibs == lax.axis_size("rad")
        and vibs > 1
        and hels > 1
        and rows % 16 == 0
        and ang % (hels * 128) == 0
        and rows * vibs <= 512
        and ang <= 1024
    )


def whole_body(older_packet, newer_packet, *rest):
    if fits(newer_packet):
        return one_vibration(older_packet, newer_packet, *rest)
    if newer_packet.shape[2] % lax.axis_size("rad") == 0:
        return by_vibration(older_packet, newer_packet, *rest)
    return body(older_packet, newer_packet, *rest)


def solution(mesh):
    return jax.shard_map(
        whole_body,
        mesh=mesh,
        in_specs=(
            P("hel", "rad", None, None),
            P("hel", "rad", None, None),
            P(),
            P("hel", None, None),
            P("rad", None, None),
            P("hel", None),
            P(),
            P("rad"),
        ),
        out_specs=(P("hel", "rad", None, None), P("hel", "rad", None, None)),
        check_vma=False,
    )
```

```python
import functools

import jax
import jax.numpy as jnp
from jax import lax
from jax.experimental import pallas as pl
from jax.experimental.pallas import tpu as pltpu
from jax.sharding import PartitionSpec as P

STEPS = 3


SCALE_FACTOR = 0.35


def from_behind(array, axis, by):
    devices = lax.axis_size(axis)
    pairs = [(i, i + by) for i in range(devices) if 0 <= i + by < devices]
    return lax.ppermute(array, axis, pairs)


def coriolis_term(block, coefs, weights):
    lower_block, lower_coefs = from_behind((block, coefs), "hel", 1)
    upper_block = from_behind(block, "hel", -1)
    below = jnp.concatenate([lower_block, block[:-1]], axis=0).astype(jnp.float32)
    below_coefs = jnp.concatenate([lower_coefs, coefs[:-1]], axis=0).astype(jnp.float32)
    above = jnp.concatenate([block[1:], upper_block], axis=0).astype(jnp.float32)
    mixed = below_coefs[:, None, :] * below + coefs.astype(jnp.float32)[:, None, :] * above
    return weights[None, :, None] * mixed


def body(
    older_packet, newer_packet, kinetic, transform, potential, coupling, radial_weight, damping
):
    hel_rows, rad_rows, vib_count, ang_count = newer_packet.shape
    flat_width = vib_count * ang_count
    rank = lax.axis_index("rad")
    previous = older_packet.reshape(hel_rows, rad_rows, flat_width)
    current = newer_packet.reshape(hel_rows, rad_rows, flat_width)
    potential_flat = potential.astype(jnp.float32).reshape(1, rad_rows * vib_count, ang_count)
    tiled_coefs = jnp.tile(coupling, (1, vib_count))
    damp = damping[None, :, None]
    for _ in range(STEPS):
        rounded = current.astype(jnp.bfloat16)
        regrouped = lax.all_to_all(rounded, "rad", split_axis=2, concat_axis=1, tiled=True)
        kinetic_term = jnp.einsum(
            "rs,ksc->krc", kinetic, regrouped, preferred_element_type=jnp.float32
        )
        returned = lax.all_to_all(kinetic_term, "rad", split_axis=1, concat_axis=2, tiled=True)
        start = rank * rad_rows
        local_weights = lax.dynamic_slice_in_dim(radial_weight, start, rad_rows, 0)
        summed = returned + coriolis_term(rounded, tiled_coefs, local_weights)
        off_grid = summed.astype(jnp.bfloat16).astype(jnp.float32)
        angular_rows = rounded.reshape(hel_rows, rad_rows * vib_count, ang_count)
        grid = jnp.einsum(
            "kna,kag->kng", angular_rows, transform, preferred_element_type=jnp.float32
        )
        grid_values = (grid * potential_flat).astype(jnp.bfloat16)
        angular_part = jnp.einsum(
            "kng,kag->kna", grid_values, transform, preferred_element_type=jnp.float32
        )
        applied = SCALE_FACTOR * (off_grid + angular_part.reshape(hel_rows, rad_rows, flat_width))
        following = damp * (2.0 * applied - damp * previous)
        previous = current
        current = following
    shape = (hel_rows, rad_rows, vib_count, ang_count)
    return (previous.reshape(shape), current.reshape(shape))


def by_vibration(
    older_packet, newer_packet, kinetic, transform, potential, coupling, radial_weight, damping
):
    hel_rows, rad_rows, vib_count, ang_count = newer_packet.shape
    devices = lax.axis_size("rad")

    def scatter(array):
        return lax.all_to_all(array, "rad", split_axis=2, concat_axis=1, tiled=True)

    rounded = scatter(newer_packet.astype(jnp.bfloat16))
    previous = scatter(older_packet.astype(jnp.bfloat16)).astype(jnp.float32)
    pot = scatter(potential[None])[0].astype(jnp.float32)
    damp = lax.all_gather(damping, "rad", tiled=True)[None, :, None, None]
    weight = radial_weight[None, :, None, None]
    current = rounded.astype(jnp.float32)
    lower_coefs = from_behind(coupling, "hel", 1)
    coefs = jnp.concatenate([lower_coefs, coupling], axis=0).astype(jnp.float32)
    coefs = coefs[:, None, None, :]
    history = []
    for step in range(STEPS):
        lower = from_behind(rounded[-1:], "hel", 1)
        upper = from_behind(rounded[:1], "hel", -1)
        padded = jnp.concatenate([lower, rounded, upper], axis=0).astype(jnp.float32)
        mixed = coefs[:-1] * padded[:-2] + coefs[1:] * padded[2:]
        radial = jnp.einsum(
            "rs,ksva->krva", kinetic, rounded, preferred_element_type=jnp.float32
        )
        off_grid = radial + weight * mixed
        grid = jnp.einsum(
            "krva,kag->krvg", rounded, transform, preferred_element_type=jnp.float32
        )
        grid_values = (grid * pot[None]).astype(jnp.bfloat16)
        angular = jnp.einsum(
            "krvg,kag->krva", grid_values, transform, preferred_element_type=jnp.float32
        )
        applied = SCALE_FACTOR * (off_grid + angular)
        following = damp * (2.0 * applied - damp * previous)
        previous = current
        current = following
        rounded = current.astype(jnp.bfloat16)
        history.append(rounded)

    def gather(array):
        back = lax.all_to_all(array, "rad", split_axis=1, concat_axis=2, tiled=True)
        return back.astype(jnp.float32)

    return gather(history[-2]), gather(history[-1])


MESH = pl.DeviceIdType.MESH
POT, NEW, OLD, DAMP, OUT3, OUT4 = range(6)


def packet_kernel(
    n, hels,
    newer, older, kinetic, transform, potential, coupling, weight, damping,
    back3, back4,
    newer_v, older_v, kin, tr, pot_in, pot_wide, coef, coef_low, damp_own, damp_all, weight_all,
    damp_col, weight_col, send_pot, send_new, send_old, pot, x0, x1, x2, x3, x4, total, grid,
    low, high,
    in_sem, lane_sem, own_sem, rad_send, rad_recv, pot_send, pot_recv, hel_send, hel_recv, coef_sem,
):
    me = lax.axis_index("rad")
    hel = lax.axis_index("hel")
    rows = send_new.shape[1]
    ang = newer.shape[1]
    width = ang // hels
    has_low = hel > 0
    has_high = hel < hels - 1

    def shift(i):
        if n % 2:
            return i + 1
        return n // 2 + ((i + 1) // 2) * (1 - 2 * (i % 2))

    def target(i):
        return lax.rem(me + shift(i), n)

    def source(i):
        return lax.rem(me - shift(i) + n, n)

    def block(c):
        return pl.ds(pl.multiple_of(c * rows, rows), rows)

    loads = [
        pltpu.make_async_copy(src, dst, in_sem.at[s])
        for s, (src, dst) in enumerate(
            (
                (potential.at[:, :, pl.ds(pl.multiple_of(hel * width, width), width)], pot_in),
                (damping, damp_own),
                (coupling, coef),
                (weight, weight_all),
                (kinetic, kin),
                (transform, tr),
            )
        )
    ]

    def lanes(l):
        return pl.ds(pl.multiple_of(l * 128, 128), 128)

    def newer_load(l):
        return pltpu.make_async_copy(newer.at[:, lanes(l)], newer_v.at[l], lane_sem.at[0, l])

    def older_load(l):
        return pltpu.make_async_copy(older.at[:, lanes(l)], older_v.at[l], lane_sem.at[1, l])

    def each_lane(copy, method):
        @pl.loop(0, ang // 128)
        def _(l):
            getattr(copy(l), method)()

    for load in loads[:3]:
        load.start()
    each_lane(newer_load, "start")
    each_lane(older_load, "start")
    for load in loads[3:]:
        load.start()

    barrier = pltpu.get_barrier_semaphore()

    @pl.loop(1, n)
    def _(j):
        pl.semaphore_signal(
            barrier, inc=1, device_id={"rad": lax.rem(me + j, n)}, device_id_type=MESH
        )

    @pl.loop(1, hels)
    def _(j):
        pl.semaphore_signal(
            barrier, inc=1, device_id={"hel": lax.rem(hel + j, hels)}, device_id_type=MESH
        )

    pl.semaphore_wait(barrier, n + hels - 2)

    def over_rad(kind, src, dst, i):
        return pltpu.make_async_remote_copy(
            src_ref=src,
            dst_ref=dst,
            send_sem=rad_send.at[kind, i],
            recv_sem=rad_recv.at[kind, i],
            device_id={"rad": target(i)},
            device_id_type=MESH,
        )

    def pot_copy(i):
        return over_rad(POT, send_pot.at[i], pot.at[hel, block(me)], i)

    def new_copy(i):
        return over_rad(NEW, send_new.at[i], x1.at[block(me)], i)

    def old_copy(i):
        return over_rad(OLD, send_old.at[i], x0.at[block(me)], i)

    def damp_copy(i):
        return over_rad(DAMP, damp_own, damp_all.at[me], i)

    def out3_copy(i):
        return over_rad(OUT3, x3.at[block(target(i))], back3.at[me], i)

    def out4_copy(i):
        return over_rad(OUT4, x4.at[block(target(i))], back4.at[me], i)

    def pot_share(j):
        return pltpu.make_async_remote_copy(
            src_ref=pot.at[hel],
            dst_ref=pot.at[hel],
            send_sem=pot_send.at[j],
            recv_sem=pot_recv.at[j],
            device_id={"hel": lax.rem(hel + j, hels)},
            device_id_type=MESH,
        )

    coef_copy = pltpu.make_async_remote_copy(
        src_ref=coef,
        dst_ref=coef_low,
        send_sem=coef_sem.at[0],
        recv_sem=coef_sem.at[1],
        device_id={"hel": lax.rem(hel + 1, hels)},
        device_id_type=MESH,
    )

    def hel_up(step, x, c, sem):
        return pltpu.make_async_remote_copy(
            src_ref=x.at[c],
            dst_ref=low.at[step, c],
            send_sem=hel_send.at[step, 0, sem],
            recv_sem=hel_recv.at[step, 0, sem],
            device_id={"hel": lax.rem(hel + 1, hels)},
            device_id_type=MESH,
        )

    def hel_down(step, x, c, sem):
        return pltpu.make_async_remote_copy(
            src_ref=x.at[c],
            dst_ref=high.at[step, c],
            send_sem=hel_send.at[step, 1, sem],
            recv_sem=hel_recv.at[step, 1, sem],
            device_id={"hel": lax.rem(hel - 1 + hels, hels)},
            device_id_type=MESH,
        )

    def hel_start(step, x, c, sem):
        @pl.when(has_high)
        def _():
            hel_up(step, x, c, sem).start()

        @pl.when(has_low)
        def _():
            hel_down(step, x, c, sem).start()

    def hel_wait_recv(step, x, c, sem):
        @pl.when(has_low)
        def _():
            hel_up(step, x, c, sem).wait_recv()

        @pl.when(has_high)
        def _():
            hel_down(step, x, c, sem).wait_recv()

    def hel_wait_send(step, x, c, sem):
        @pl.when(has_high)
        def _():
            hel_up(step, x, c, sem).wait_send()

        @pl.when(has_low)
        def _():
            hel_down(step, x, c, sem).wait_send()

    def trailing(make, copy):
        @pl.loop(0, n - 1)
        def _(i):
            make(i)

            @pl.when(i > 0)
            def _():
                copy(i - 1).start()

    everything = pl.ds(0, n * rows)

    loads[0].wait()
    for l in range(width // 128):
        part = pot_in[:, :, 128 * l : 128 * (l + 1)].astype(jnp.float32)
        pot_wide[l] = part.reshape(pot_wide.shape[1:])

    def picked(ref, c):
        return jnp.concatenate(
            [
                ref[l, pl.ds(c, rows, stride=n), :]
                for l in range(ref.shape[0])
            ],
            axis=1,
        ).astype(jnp.bfloat16)

    def make_pot(i):
        send_pot[i] = picked(pot_wide, target(i))

    trailing(make_pot, pot_copy)
    pot[hel, block(me)] = picked(pot_wide, me)
    pot_copy(n - 2).start()

    each_lane(newer_load, "wait")

    def make_new(i):
        send_new[i] = picked(newer_v, target(i))

    trailing(make_new, new_copy)
    x1[block(me)] = picked(newer_v, me)
    new_copy(n - 2).start()

    loads[1].wait()
    loads[2].wait()

    @pl.loop(0, n - 1)
    def _(i):
        damp_copy(i).start()

    @pl.when(has_high)
    def _():
        coef_copy.start()

    each_lane(older_load, "wait")

    def make_old(i):
        send_old[i] = picked(older_v, target(i))

    trailing(make_old, old_copy)
    x0[block(me)] = picked(older_v, me)
    old_copy(n - 2).start()
    damp_all[me] = damp_own[...]

    @pl.when(jnp.logical_not(has_low))
    def _():
        low[...] = jnp.zeros_like(low)
        coef_low[...] = jnp.zeros_like(coef_low)

    @pl.when(jnp.logical_not(has_high))
    def _():
        high[...] = jnp.zeros_like(high)

    for load in loads[3:]:
        load.wait()

    @pl.loop(0, n - 1)
    def _(i):
        pot_copy(i).wait_recv()

    @pl.loop(1, hels)
    def _(j):
        pot_share(j).start()

    @pl.loop(0, n - 1)
    def _(i):
        damp_copy(i).wait_recv()

    @pl.when(has_low)
    def _():
        coef_copy.wait_recv()

    line = lax.broadcasted_iota(jnp.int32, (rows, rows), 0)
    lane = lax.broadcasted_iota(jnp.int32, (rows, rows), 1)

    def column(row):
        diagonal = jnp.where(line == lane, jnp.broadcast_to(row, (rows, rows)), 0.0)
        return jnp.broadcast_to(jnp.sum(diagonal, axis=1, keepdims=True), (rows, 128))

    @pl.loop(0, n)
    def _(c):
        damp_col[block(c)] = column(damp_all[c])

    for c in range(n):
        part = weight_all[:, c * rows : (c + 1) * rows]
        weight_col[c * rows : (c + 1) * rows] = column(part)

    hel_start(0, x1, block(me), 0)

    @pl.loop(0, n - 1)
    def _(i):
        new_copy(i).wait_recv()
        hel_start(0, x1, block(source(i)), n - shift(i))

    @pl.loop(1, hels)
    def _(j):
        pot_share(j).wait_recv()

    def tile(t):
        return pl.ds(pl.multiple_of(t * width, width), width)

    def angular_block(x, span, between):
        @pl.loop(0, hels)
        def _(t):
            values = jnp.dot(x[span], tr[:, tile(t)], preferred_element_type=jnp.float32)
            values = values * pot[t, span].astype(jnp.float32)
            grid[span, tile(t)] = values.astype(jnp.bfloat16)

        between()

        @pl.loop(0, hels)
        def _(t):
            total[span, tile(t)] = lax.dot_general(
                grid[span],
                tr[tile(t), :],
                (((1,), (1,)), ((), ())),
                preferred_element_type=jnp.float32,
            )

    def multiply(x):
        @pl.loop(0, hels)
        def _(t):
            values = jnp.dot(x[...], tr[:, tile(t)], preferred_element_type=jnp.float32)
            grid[:, tile(t)] = (values * pot[t].astype(jnp.float32)).astype(jnp.bfloat16)

        @pl.loop(0, hels)
        def _(t):
            radial = jnp.dot(kin[...], x[:, tile(t)], preferred_element_type=jnp.float32)
            angular = lax.dot_general(
                grid[...],
                tr[tile(t), :],
                (((1,), (1,)), ((), ())),
                preferred_element_type=jnp.float32,
            )
            total[:, tile(t)] = radial + angular

    lower_coef = coef_low[...].astype(jnp.float32)
    upper_coef = coef[...].astype(jnp.float32)

    def finish(step, prev, c):
        span = block(c)
        damp = damp_col[span, 0:1]
        mixed = lower_coef * low[step, span].astype(jnp.float32)
        mixed = mixed + upper_coef * high[step, span].astype(jnp.float32)
        applied = SCALE_FACTOR * (total[span] + weight_col[span, 0:1] * mixed)
        following = damp * (2.0 * applied - damp * prev[span].astype(jnp.float32))
        return following.astype(jnp.bfloat16)

    multiply(x1)

    def hel_arrived(step, x):
        @pl.loop(0, n)
        def _(i):
            hel_wait_recv(step, x, block(lax.rem(me + i, n)), i)

    hel_arrived(0, x1)

    def next_block(c, sem):
        x2[block(c)] = finish(0, x0, c)
        angular_block(x2, block(c), lambda: hel_start(1, x2, block(c), sem))

    next_block(me, 0)

    @pl.loop(0, n - 1)
    def _(i):
        old_copy(i).wait_recv()
        next_block(source(i), n - shift(i))

    @pl.loop(0, hels)
    def _(t):
        total[:, tile(t)] += jnp.dot(
            kin[...], x2[:, tile(t)], preferred_element_type=jnp.float32
        )

    hel_arrived(1, x2)

    def make_out3(i):
        x3[block(target(i))] = finish(1, x1, target(i))

    trailing(make_out3, out3_copy)
    x3[block(me)] = finish(1, x1, me)
    out3_copy(n - 2).start()
    hel_start(2, x3, everything, 0)

    multiply(x3)
    hel_wait_recv(2, x3, everything, 0)

    def make_out4(i):
        x4[block(target(i))] = finish(2, x2, target(i))

    trailing(make_out4, out4_copy)
    x4[block(me)] = finish(2, x2, me)
    out4_copy(n - 2).start()

    own = [
        pltpu.make_async_copy(x.at[block(me)], back.at[me], own_sem.at[j])
        for j, (x, back) in enumerate(((x3, back3), (x4, back4)))
    ]
    for copy in own:
        copy.start()

    @pl.loop(0, n - 1)
    def _(i):
        out3_copy(i).wait_recv()
        out4_copy(i).wait_recv()

    @pl.loop(0, n - 1)
    def _(i):
        for copy in (pot_copy, new_copy, old_copy, damp_copy, out3_copy, out4_copy):
            copy(i).wait_send()

    @pl.loop(1, hels)
    def _(j):
        pot_share(j).wait_send()

    @pl.when(has_high)
    def _():
        coef_copy.wait_send()

    hel_wait_send(2, x3, everything, 0)

    @pl.loop(0, n)
    def _(i):
        hel_wait_send(0, x1, block(lax.rem(me + i, n)), i)
        hel_wait_send(1, x2, block(lax.rem(me + i, n)), i)

    for copy in own:
        copy.wait()


def place_kernel(n, back3, back4, out_old, out_new, held, wide, in_sem, out_sem):
    rows, ang = back3.shape[1:]
    groups = ang // 128
    pairs = ((back3, out_old), (back4, out_new))

    def load(s, l):
        return pltpu.make_async_copy(
            pairs[s][0].at[:, :, pl.ds(128 * l, 128)], held.at[s, l], in_sem.at[s, l]
        )

    def unload(s, l):
        return pltpu.make_async_copy(
            wide.at[s, l], pairs[s][1].at[:, pl.ds(128 * l, 128)], out_sem.at[s, l]
        )

    every = [(s, l) for s in range(2) for l in range(groups)]
    for s, l in every:
        load(s, l).start()
    for s, l in every:
        load(s, l).wait()
        for c in range(n):
            wide[s, l, pl.ds(c, rows, stride=n), :] = held[s, l, c].astype(jnp.float32)
        unload(s, l).start()
    for s, l in every:
        unload(s, l).wait()


def one_vibration(
    older_packet, newer_packet, kinetic, transform, potential, coupling, radial_weight, damping
):
    _, rows, n, ang = newer_packet.shape
    hels = lax.axis_size("hel")
    width = ang // hels
    points = n * rows
    bf16, f32 = jnp.bfloat16, jnp.float32
    vector = pltpu.VMEM((points, ang), bf16)
    blocks = pltpu.VMEM((n, rows, ang), bf16)
    wide = pltpu.VMEM((points, ang), f32)
    flat = jax.ShapeDtypeStruct((points, ang), f32)
    back = jax.ShapeDtypeStruct((n, rows, ang), bf16)
    anywhere = pl.BlockSpec(memory_space=pl.ANY)
    sem = pltpu.SemaphoreType.DMA
    groups = ang // 128
    backs = pl.pallas_call(
        functools.partial(packet_kernel, n, hels),
        out_shape=(back, back),
        in_specs=[anywhere] * 8,
        out_specs=(anywhere, anywhere),
        scratch_shapes=[
            pltpu.VMEM((ang // 128, points, 128), f32),
            pltpu.VMEM((ang // 128, points, 128), f32),
            pltpu.VMEM((points, points), bf16),
            pltpu.VMEM((ang, ang), bf16),
            pltpu.VMEM((rows, n, width), bf16),
            pltpu.VMEM((width // 128, points, 128), f32),
            pltpu.VMEM((1, ang), bf16),
            pltpu.VMEM((1, ang), bf16),
            pltpu.VMEM((1, rows), f32),
            pltpu.VMEM((n, 1, rows), f32),
            pltpu.VMEM((1, points), f32),
            pltpu.VMEM((points, 128), f32),
            pltpu.VMEM((points, 128), f32),
            pltpu.VMEM((n, rows, width), bf16),
            blocks,
            blocks,
            pltpu.VMEM((hels, points, width), bf16),
            vector,
            vector,
            vector,
            vector,
            vector,
            wide,
            vector,
            pltpu.VMEM((STEPS, points, ang), bf16),
            pltpu.VMEM((STEPS, points, ang), bf16),
            sem((6,)),
            sem((2, groups)),
            sem((2,)),
            sem((6, n)),
            sem((6, n)),
            sem((hels,)),
            sem((hels,)),
            sem((STEPS, 2, n)),
            sem((STEPS, 2, n)),
            sem((2,)),
        ],
        compiler_params=pltpu.CompilerParams(
            collective_id=0, has_side_effects=True, vmem_limit_bytes=60 * 1024 * 1024
        ),
    )(
        newer_packet.reshape(points, ang),
        older_packet.reshape(points, ang),
        kinetic,
        transform[0],
        potential,
        coupling,
        radial_weight.reshape(1, points),
        damping.reshape(1, rows),
    )
    outs = pl.pallas_call(
        functools.partial(place_kernel, n),
        out_shape=(flat, flat),
        in_specs=[anywhere] * 2,
        out_specs=(anywhere, anywhere),
        scratch_shapes=[
            pltpu.VMEM((2, groups, n, rows, 128), bf16),
            pltpu.VMEM((2, groups, points, 128), f32),
            sem((2, groups)),
            sem((2, groups)),
        ],
    )(*backs)
    shape = newer_packet.shape
    return outs[0].reshape(shape), outs[1].reshape(shape)


def fits(packet):
    hel_rows, rows, vibs, ang = packet.shape
    hels = lax.axis_size("hel")
    return (
        STEPS == 3
        and hel_rows == 1
        and vibs == lax.axis_size("rad")
        and vibs > 1
        and hels > 1
        and rows % 16 == 0
        and ang % (hels * 128) == 0
        and rows * vibs <= 512
        and ang <= 1024
    )


def whole_body(older_packet, newer_packet, *rest):
    if fits(newer_packet):
        return one_vibration(older_packet, newer_packet, *rest)
    if newer_packet.shape[2] % lax.axis_size("rad") == 0:
        return by_vibration(older_packet, newer_packet, *rest)
    return body(older_packet, newer_packet, *rest)


def solution(mesh):
    return jax.shard_map(
        whole_body,
        mesh=mesh,
        in_specs=(
            P("hel", "rad", None, None),
            P("hel", "rad", None, None),
            P(),
            P("hel", None, None),
            P("rad", None, None),
            P("hel", None),
            P(),
            P("rad"),
        ),
        out_specs=(P("hel", "rad", None, None), P("hel", "rad", None, None)),
        check_vma=False,
    )
```

```python
import functools

import jax
import jax.numpy as jnp
from jax import lax
from jax.experimental import pallas as pl
from jax.experimental.pallas import tpu as pltpu
from jax.sharding import PartitionSpec as P

STEPS = 3


SCALE_FACTOR = 0.35


def from_behind(array, axis, by):
    devices = lax.axis_size(axis)
    pairs = [(i, i + by) for i in range(devices) if 0 <= i + by < devices]
    return lax.ppermute(array, axis, pairs)


def coriolis_term(block, coefs, weights):
    lower_block, lower_coefs = from_behind((block, coefs), "hel", 1)
    upper_block = from_behind(block, "hel", -1)
    below = jnp.concatenate([lower_block, block[:-1]], axis=0).astype(jnp.float32)
    below_coefs = jnp.concatenate([lower_coefs, coefs[:-1]], axis=0).astype(jnp.float32)
    above = jnp.concatenate([block[1:], upper_block], axis=0).astype(jnp.float32)
    mixed = below_coefs[:, None, :] * below + coefs.astype(jnp.float32)[:, None, :] * above
    return weights[None, :, None] * mixed


def body(
    older_packet, newer_packet, kinetic, transform, potential, coupling, radial_weight, damping
):
    hel_rows, rad_rows, vib_count, ang_count = newer_packet.shape
    flat_width = vib_count * ang_count
    rank = lax.axis_index("rad")
    previous = older_packet.reshape(hel_rows, rad_rows, flat_width)
    current = newer_packet.reshape(hel_rows, rad_rows, flat_width)
    potential_flat = potential.astype(jnp.float32).reshape(1, rad_rows * vib_count, ang_count)
    tiled_coefs = jnp.tile(coupling, (1, vib_count))
    damp = damping[None, :, None]
    for _ in range(STEPS):
        rounded = current.astype(jnp.bfloat16)
        regrouped = lax.all_to_all(rounded, "rad", split_axis=2, concat_axis=1, tiled=True)
        kinetic_term = jnp.einsum(
            "rs,ksc->krc", kinetic, regrouped, preferred_element_type=jnp.float32
        )
        returned = lax.all_to_all(kinetic_term, "rad", split_axis=1, concat_axis=2, tiled=True)
        start = rank * rad_rows
        local_weights = lax.dynamic_slice_in_dim(radial_weight, start, rad_rows, 0)
        summed = returned + coriolis_term(rounded, tiled_coefs, local_weights)
        off_grid = summed.astype(jnp.bfloat16).astype(jnp.float32)
        angular_rows = rounded.reshape(hel_rows, rad_rows * vib_count, ang_count)
        grid = jnp.einsum(
            "kna,kag->kng", angular_rows, transform, preferred_element_type=jnp.float32
        )
        grid_values = (grid * potential_flat).astype(jnp.bfloat16)
        angular_part = jnp.einsum(
            "kng,kag->kna", grid_values, transform, preferred_element_type=jnp.float32
        )
        applied = SCALE_FACTOR * (off_grid + angular_part.reshape(hel_rows, rad_rows, flat_width))
        following = damp * (2.0 * applied - damp * previous)
        previous = current
        current = following
    shape = (hel_rows, rad_rows, vib_count, ang_count)
    return (previous.reshape(shape), current.reshape(shape))


def by_vibration(
    older_packet, newer_packet, kinetic, transform, potential, coupling, radial_weight, damping
):
    hel_rows, rad_rows, vib_count, ang_count = newer_packet.shape
    devices = lax.axis_size("rad")

    def scatter(array):
        return lax.all_to_all(array, "rad", split_axis=2, concat_axis=1, tiled=True)

    rounded = scatter(newer_packet.astype(jnp.bfloat16))
    previous = scatter(older_packet.astype(jnp.bfloat16)).astype(jnp.float32)
    pot = scatter(potential[None])[0].astype(jnp.float32)
    damp = lax.all_gather(damping, "rad", tiled=True)[None, :, None, None]
    weight = radial_weight[None, :, None, None]
    current = rounded.astype(jnp.float32)
    lower_coefs = from_behind(coupling, "hel", 1)
    coefs = jnp.concatenate([lower_coefs, coupling], axis=0).astype(jnp.float32)
    coefs = coefs[:, None, None, :]
    history = []
    for step in range(STEPS):
        lower = from_behind(rounded[-1:], "hel", 1)
        upper = from_behind(rounded[:1], "hel", -1)
        padded = jnp.concatenate([lower, rounded, upper], axis=0).astype(jnp.float32)
        mixed = coefs[:-1] * padded[:-2] + coefs[1:] * padded[2:]
        radial = jnp.einsum(
            "rs,ksva->krva", kinetic, rounded, preferred_element_type=jnp.float32
        )
        off_grid = radial + weight * mixed
        grid = jnp.einsum(
            "krva,kag->krvg", rounded, transform, preferred_element_type=jnp.float32
        )
        grid_values = (grid * pot[None]).astype(jnp.bfloat16)
        angular = jnp.einsum(
            "krvg,kag->krva", grid_values, transform, preferred_element_type=jnp.float32
        )
        applied = SCALE_FACTOR * (off_grid + angular)
        following = damp * (2.0 * applied - damp * previous)
        previous = current
        current = following
        rounded = current.astype(jnp.bfloat16)
        history.append(rounded)

    def gather(array):
        back = lax.all_to_all(array, "rad", split_axis=1, concat_axis=2, tiled=True)
        return back.astype(jnp.float32)

    return gather(history[-2]), gather(history[-1])


MESH = pl.DeviceIdType.MESH
POT, NEW, OLD, DAMP, OUT3, OUT4 = range(6)


def packet_kernel(
    n, hels,
    newer, older, kinetic, transform, potential, coupling, weight, damping,
    back3, back4,
    newer_v, older_v, kin, tr, pot_in, pot_wide, coef, coef_low, damp_own, damp_all, weight_all,
    damp_col, weight_col, send_pot, send_new, send_old, pot, x0, x1, x2, x3, x4, total, grid,
    low, high,
    in_sem, lane_sem, own_sem, rad_send, rad_recv, pot_send, pot_recv, hel_send, hel_recv, coef_sem,
):
    me = lax.axis_index("rad")
    hel = lax.axis_index("hel")
    rows = send_new.shape[1]
    ang = newer.shape[1]
    width = ang // hels
    has_low = hel > 0
    has_high = hel < hels - 1

    def shift(i):
        if n % 2:
            return i + 1
        return n // 2 + ((i + 1) // 2) * (1 - 2 * (i % 2))

    def target(i):
        return lax.rem(me + shift(i), n)

    def source(i):
        return lax.rem(me - shift(i) + n, n)

    def block(c):
        return pl.ds(pl.multiple_of(c * rows, rows), rows)

    loads = [
        pltpu.make_async_copy(src, dst, in_sem.at[s])
        for s, (src, dst) in enumerate(
            (
                (potential.at[:, :, pl.ds(pl.multiple_of(hel * width, width), width)], pot_in),
                (damping, damp_own),
                (coupling, coef),
                (weight, weight_all),
                (kinetic, kin),
                (transform, tr),
            )
        )
    ]

    def lanes(l):
        return pl.ds(pl.multiple_of(l * 128, 128), 128)

    def newer_load(l):
        return pltpu.make_async_copy(newer.at[:, lanes(l)], newer_v.at[l], lane_sem.at[0, l])

    def older_load(l):
        return pltpu.make_async_copy(older.at[:, lanes(l)], older_v.at[l], lane_sem.at[1, l])

    def each_lane(copy, method):
        @pl.loop(0, ang // 128)
        def _(l):
            getattr(copy(l), method)()

    for load in loads[:3]:
        load.start()
    each_lane(newer_load, "start")
    each_lane(older_load, "start")
    for load in loads[3:]:
        load.start()

    barrier = pltpu.get_barrier_semaphore()

    @pl.loop(1, n)
    def _(j):
        pl.semaphore_signal(
            barrier, inc=1, device_id={"rad": lax.rem(me + j, n)}, device_id_type=MESH
        )

    @pl.loop(1, hels)
    def _(j):
        pl.semaphore_signal(
            barrier, inc=1, device_id={"hel": lax.rem(hel + j, hels)}, device_id_type=MESH
        )

    pl.semaphore_wait(barrier, n + hels - 2)

    def over_rad(kind, src, dst, i):
        return pltpu.make_async_remote_copy(
            src_ref=src,
            dst_ref=dst,
            send_sem=rad_send.at[kind, i],
            recv_sem=rad_recv.at[kind, i],
            device_id={"rad": target(i)},
            device_id_type=MESH,
        )

    def pot_copy(i):
        return over_rad(POT, send_pot.at[i], pot.at[hel, block(me)], i)

    def new_copy(i):
        return over_rad(NEW, send_new.at[i], x1.at[block(me)], i)

    def old_copy(i):
        return over_rad(OLD, send_old.at[i], x0.at[block(me)], i)

    def damp_copy(i):
        return over_rad(DAMP, damp_own, damp_all.at[me], i)

    def out3_copy(i):
        return over_rad(OUT3, x3.at[block(target(i))], back3.at[me], i)

    def out4_copy(i):
        return over_rad(OUT4, x4.at[block(target(i))], back4.at[me], i)

    def pot_share(j):
        return pltpu.make_async_remote_copy(
            src_ref=pot.at[hel],
            dst_ref=pot.at[hel],
            send_sem=pot_send.at[j],
            recv_sem=pot_recv.at[j],
            device_id={"hel": lax.rem(hel + j, hels)},
            device_id_type=MESH,
        )

    coef_copy = pltpu.make_async_remote_copy(
        src_ref=coef,
        dst_ref=coef_low,
        send_sem=coef_sem.at[0],
        recv_sem=coef_sem.at[1],
        device_id={"hel": lax.rem(hel + 1, hels)},
        device_id_type=MESH,
    )

    def hel_up(step, x, c, sem):
        return pltpu.make_async_remote_copy(
            src_ref=x.at[c],
            dst_ref=low.at[step, c],
            send_sem=hel_send.at[step, 0, sem],
            recv_sem=hel_recv.at[step, 0, sem],
            device_id={"hel": lax.rem(hel + 1, hels)},
            device_id_type=MESH,
        )

    def hel_down(step, x, c, sem):
        return pltpu.make_async_remote_copy(
            src_ref=x.at[c],
            dst_ref=high.at[step, c],
            send_sem=hel_send.at[step, 1, sem],
            recv_sem=hel_recv.at[step, 1, sem],
            device_id={"hel": lax.rem(hel - 1 + hels, hels)},
            device_id_type=MESH,
        )

    def hel_start(step, x, c, sem):
        @pl.when(has_high)
        def _():
            hel_up(step, x, c, sem).start()

        @pl.when(has_low)
        def _():
            hel_down(step, x, c, sem).start()

    def hel_wait_recv(step, x, c, sem):
        @pl.when(has_low)
        def _():
            hel_up(step, x, c, sem).wait_recv()

        @pl.when(has_high)
        def _():
            hel_down(step, x, c, sem).wait_recv()

    def hel_wait_send(step, x, c, sem):
        @pl.when(has_high)
        def _():
            hel_up(step, x, c, sem).wait_send()

        @pl.when(has_low)
        def _():
            hel_down(step, x, c, sem).wait_send()

    def trailing(make, copy):
        @pl.loop(0, n - 1)
        def _(i):
            make(i)

            @pl.when(i > 0)
            def _():
                copy(i - 1).start()

    everything = pl.ds(0, n * rows)

    loads[0].wait()
    for l in range(width // 128):
        part = pot_in[:, :, 128 * l : 128 * (l + 1)].astype(jnp.float32)
        pot_wide[l] = part.reshape(pot_wide.shape[1:])

    def picked(ref, c):
        return jnp.concatenate(
            [
                ref[l, pl.ds(c, rows, stride=n), :]
                for l in range(ref.shape[0])
            ],
            axis=1,
        ).astype(jnp.bfloat16)

    def make_pot(i):
        send_pot[i] = picked(pot_wide, target(i))

    trailing(make_pot, pot_copy)
    pot[hel, block(me)] = picked(pot_wide, me)
    pot_copy(n - 2).start()

    each_lane(newer_load, "wait")

    def make_new(i):
        send_new[i] = picked(newer_v, target(i))

    trailing(make_new, new_copy)
    x1[block(me)] = picked(newer_v, me)
    new_copy(n - 2).start()

    loads[1].wait()
    loads[2].wait()

    @pl.loop(0, n - 1)
    def _(i):
        damp_copy(i).start()

    @pl.when(has_high)
    def _():
        coef_copy.start()

    each_lane(older_load, "wait")

    def make_old(i):
        send_old[i] = picked(older_v, target(i))

    trailing(make_old, old_copy)
    x0[block(me)] = picked(older_v, me)
    old_copy(n - 2).start()
    damp_all[me] = damp_own[...]

    @pl.when(jnp.logical_not(has_low))
    def _():
        low[...] = jnp.zeros_like(low)
        coef_low[...] = jnp.zeros_like(coef_low)

    @pl.when(jnp.logical_not(has_high))
    def _():
        high[...] = jnp.zeros_like(high)

    for load in loads[3:]:
        load.wait()

    @pl.loop(0, n - 1)
    def _(i):
        pot_copy(i).wait_recv()

    @pl.loop(1, hels)
    def _(j):
        pot_share(j).start()

    @pl.loop(0, n - 1)
    def _(i):
        damp_copy(i).wait_recv()

    @pl.when(has_low)
    def _():
        coef_copy.wait_recv()

    line = lax.broadcasted_iota(jnp.int32, (rows, rows), 0)
    lane = lax.broadcasted_iota(jnp.int32, (rows, rows), 1)

    def column(row):
        diagonal = jnp.where(line == lane, jnp.broadcast_to(row, (rows, rows)), 0.0)
        return jnp.broadcast_to(jnp.sum(diagonal, axis=1, keepdims=True), (rows, 128))

    @pl.loop(0, n)
    def _(c):
        damp_col[block(c)] = column(damp_all[c])

    for c in range(n):
        part = weight_all[:, c * rows : (c + 1) * rows]
        weight_col[c * rows : (c + 1) * rows] = column(part)

    hel_start(0, x1, block(me), 0)

    @pl.loop(0, n - 1)
    def _(i):
        new_copy(i).wait_recv()
        hel_start(0, x1, block(source(i)), n - shift(i))

    @pl.loop(1, hels)
    def _(j):
        pot_share(j).wait_recv()

    def to_grid(x, span):
        values = jnp.dot(x[span], tr[...], preferred_element_type=jnp.float32)
        for t in range(hels):
            part = values[:, t * width : (t + 1) * width] * pot[t, span].astype(jnp.float32)
            grid[span, t * width : (t + 1) * width] = part.astype(jnp.bfloat16)

    def from_grid(span):
        return lax.dot_general(
            grid[span], tr[...], (((1,), (1,)), ((), ())), preferred_element_type=jnp.float32
        )

    def radial(x):
        return jnp.dot(kin[...], x[...], preferred_element_type=jnp.float32)

    def multiply(x):
        to_grid(x, everything)
        total[...] = from_grid(everything) + radial(x)

    lower_coef = coef_low[...].astype(jnp.float32)
    upper_coef = coef[...].astype(jnp.float32)

    def finish(step, prev, c):
        span = block(c)
        damp = damp_col[span, 0:1]
        mixed = lower_coef * low[step, span].astype(jnp.float32)
        mixed = mixed + upper_coef * high[step, span].astype(jnp.float32)
        applied = SCALE_FACTOR * (total[span] + weight_col[span, 0:1] * mixed)
        following = damp * (2.0 * applied - damp * prev[span].astype(jnp.float32))
        return following.astype(jnp.bfloat16)

    multiply(x1)

    def hel_arrived(step, x):
        @pl.loop(0, n)
        def _(i):
            hel_wait_recv(step, x, block(lax.rem(me + i, n)), i)

    hel_arrived(0, x1)

    def next_block(c, sem):
        x2[block(c)] = finish(0, x0, c)
        to_grid(x2, block(c))
        hel_start(1, x2, block(c), sem)
        total[block(c)] = from_grid(block(c))

    next_block(me, 0)

    @pl.loop(0, n - 1)
    def _(i):
        old_copy(i).wait_recv()
        next_block(source(i), n - shift(i))

    total[...] += radial(x2)
    hel_arrived(1, x2)

    def make_out3(i):
        x3[block(target(i))] = finish(1, x1, target(i))

    trailing(make_out3, out3_copy)
    x3[block(me)] = finish(1, x1, me)
    out3_copy(n - 2).start()
    hel_start(2, x3, everything, 0)

    multiply(x3)
    hel_wait_recv(2, x3, everything, 0)

    def make_out4(i):
        x4[block(target(i))] = finish(2, x2, target(i))

    trailing(make_out4, out4_copy)
    x4[block(me)] = finish(2, x2, me)
    out4_copy(n - 2).start()

    own = [
        pltpu.make_async_copy(x.at[block(me)], back.at[me], own_sem.at[j])
        for j, (x, back) in enumerate(((x3, back3), (x4, back4)))
    ]
    for copy in own:
        copy.start()

    @pl.loop(0, n - 1)
    def _(i):
        out3_copy(i).wait_recv()
        out4_copy(i).wait_recv()

    @pl.loop(0, n - 1)
    def _(i):
        for copy in (pot_copy, new_copy, old_copy, damp_copy, out3_copy, out4_copy):
            copy(i).wait_send()

    @pl.loop(1, hels)
    def _(j):
        pot_share(j).wait_send()

    @pl.when(has_high)
    def _():
        coef_copy.wait_send()

    hel_wait_send(2, x3, everything, 0)

    @pl.loop(0, n)
    def _(i):
        hel_wait_send(0, x1, block(lax.rem(me + i, n)), i)
        hel_wait_send(1, x2, block(lax.rem(me + i, n)), i)

    for copy in own:
        copy.wait()


def place_kernel(n, back3, back4, out_old, out_new, held, wide, in_sem, out_sem):
    rows, ang = back3.shape[1:]
    groups = ang // 128
    pairs = ((back3, out_old), (back4, out_new))

    def load(s, l):
        return pltpu.make_async_copy(
            pairs[s][0].at[:, :, pl.ds(128 * l, 128)], held.at[s, l], in_sem.at[s, l]
        )

    def unload(s, l):
        return pltpu.make_async_copy(
            wide.at[s, l], pairs[s][1].at[:, pl.ds(128 * l, 128)], out_sem.at[s, l]
        )

    every = [(s, l) for s in range(2) for l in range(groups)]
    for s, l in every:
        load(s, l).start()
    for s, l in every:
        load(s, l).wait()
        for c in range(n):
            wide[s, l, pl.ds(c, rows, stride=n), :] = held[s, l, c].astype(jnp.float32)
        unload(s, l).start()
    for s, l in every:
        unload(s, l).wait()


def one_vibration(
    older_packet, newer_packet, kinetic, transform, potential, coupling, radial_weight, damping
):
    _, rows, n, ang = newer_packet.shape
    hels = lax.axis_size("hel")
    width = ang // hels
    points = n * rows
    bf16, f32 = jnp.bfloat16, jnp.float32
    vector = pltpu.VMEM((points, ang), bf16)
    blocks = pltpu.VMEM((n, rows, ang), bf16)
    wide = pltpu.VMEM((points, ang), f32)
    flat = jax.ShapeDtypeStruct((points, ang), f32)
    back = jax.ShapeDtypeStruct((n, rows, ang), bf16)
    anywhere = pl.BlockSpec(memory_space=pl.ANY)
    sem = pltpu.SemaphoreType.DMA
    groups = ang // 128
    backs = pl.pallas_call(
        functools.partial(packet_kernel, n, hels),
        out_shape=(back, back),
        in_specs=[anywhere] * 8,
        out_specs=(anywhere, anywhere),
        scratch_shapes=[
            pltpu.VMEM((ang // 128, points, 128), f32),
            pltpu.VMEM((ang // 128, points, 128), f32),
            pltpu.VMEM((points, points), bf16),
            pltpu.VMEM((ang, ang), bf16),
            pltpu.VMEM((rows, n, width), bf16),
            pltpu.VMEM((width // 128, points, 128), f32),
            pltpu.VMEM((1, ang), bf16),
            pltpu.VMEM((1, ang), bf16),
            pltpu.VMEM((1, rows), f32),
            pltpu.VMEM((n, 1, rows), f32),
            pltpu.VMEM((1, points), f32),
            pltpu.VMEM((points, 128), f32),
            pltpu.VMEM((points, 128), f32),
            pltpu.VMEM((n, rows, width), bf16),
            blocks,
            blocks,
            pltpu.VMEM((hels, points, width), bf16),
            vector,
            vector,
            vector,
            vector,
            vector,
            wide,
            vector,
            pltpu.VMEM((STEPS, points, ang), bf16),
            pltpu.VMEM((STEPS, points, ang), bf16),
            sem((6,)),
            sem((2, groups)),
            sem((2,)),
            sem((6, n)),
            sem((6, n)),
            sem((hels,)),
            sem((hels,)),
            sem((STEPS, 2, n)),
            sem((STEPS, 2, n)),
            sem((2,)),
        ],
        compiler_params=pltpu.CompilerParams(
            collective_id=0, has_side_effects=True, vmem_limit_bytes=60 * 1024 * 1024
        ),
    )(
        newer_packet.reshape(points, ang),
        older_packet.reshape(points, ang),
        kinetic,
        transform[0],
        potential,
        coupling,
        radial_weight.reshape(1, points),
        damping.reshape(1, rows),
    )
    outs = pl.pallas_call(
        functools.partial(place_kernel, n),
        out_shape=(flat, flat),
        in_specs=[anywhere] * 2,
        out_specs=(anywhere, anywhere),
        scratch_shapes=[
            pltpu.VMEM((2, groups, n, rows, 128), bf16),
            pltpu.VMEM((2, groups, points, 128), f32),
            sem((2, groups)),
            sem((2, groups)),
        ],
    )(*backs)
    shape = newer_packet.shape
    return outs[0].reshape(shape), outs[1].reshape(shape)


def fits(packet):
    hel_rows, rows, vibs, ang = packet.shape
    hels = lax.axis_size("hel")
    return (
        STEPS == 3
        and hel_rows == 1
        and vibs == lax.axis_size("rad")
        and vibs > 1
        and hels > 1
        and rows % 16 == 0
        and ang % (hels * 128) == 0
        and rows * vibs <= 512
        and ang <= 1024
    )


def whole_body(older_packet, newer_packet, *rest):
    if fits(newer_packet):
        return one_vibration(older_packet, newer_packet, *rest)
    if newer_packet.shape[2] % lax.axis_size("rad") == 0:
        return by_vibration(older_packet, newer_packet, *rest)
    return body(older_packet, newer_packet, *rest)


def solution(mesh):
    return jax.shard_map(
        whole_body,
        mesh=mesh,
        in_specs=(
            P("hel", "rad", None, None),
            P("hel", "rad", None, None),
            P(),
            P("hel", None, None),
            P("rad", None, None),
            P("hel", None),
            P(),
            P("rad"),
        ),
        out_specs=(P("hel", "rad", None, None), P("hel", "rad", None, None)),
        check_vma=False,
    )
```

```python
import functools

import jax
import jax.numpy as jnp
from jax import lax
from jax.experimental import pallas as pl
from jax.experimental.pallas import tpu as pltpu
from jax.sharding import PartitionSpec as P

STEPS = 3


SCALE_FACTOR = 0.35


def from_behind(array, axis, by):
    devices = lax.axis_size(axis)
    pairs = [(i, i + by) for i in range(devices) if 0 <= i + by < devices]
    return lax.ppermute(array, axis, pairs)


def coriolis_term(block, coefs, weights):
    lower_block, lower_coefs = from_behind((block, coefs), "hel", 1)
    upper_block = from_behind(block, "hel", -1)
    below = jnp.concatenate([lower_block, block[:-1]], axis=0).astype(jnp.float32)
    below_coefs = jnp.concatenate([lower_coefs, coefs[:-1]], axis=0).astype(jnp.float32)
    above = jnp.concatenate([block[1:], upper_block], axis=0).astype(jnp.float32)
    mixed = below_coefs[:, None, :] * below + coefs.astype(jnp.float32)[:, None, :] * above
    return weights[None, :, None] * mixed


def body(
    older_packet, newer_packet, kinetic, transform, potential, coupling, radial_weight, damping
):
    hel_rows, rad_rows, vib_count, ang_count = newer_packet.shape
    flat_width = vib_count * ang_count
    rank = lax.axis_index("rad")
    previous = older_packet.reshape(hel_rows, rad_rows, flat_width)
    current = newer_packet.reshape(hel_rows, rad_rows, flat_width)
    potential_flat = potential.astype(jnp.float32).reshape(1, rad_rows * vib_count, ang_count)
    tiled_coefs = jnp.tile(coupling, (1, vib_count))
    damp = damping[None, :, None]
    for _ in range(STEPS):
        rounded = current.astype(jnp.bfloat16)
        regrouped = lax.all_to_all(rounded, "rad", split_axis=2, concat_axis=1, tiled=True)
        kinetic_term = jnp.einsum(
            "rs,ksc->krc", kinetic, regrouped, preferred_element_type=jnp.float32
        )
        returned = lax.all_to_all(kinetic_term, "rad", split_axis=1, concat_axis=2, tiled=True)
        start = rank * rad_rows
        local_weights = lax.dynamic_slice_in_dim(radial_weight, start, rad_rows, 0)
        summed = returned + coriolis_term(rounded, tiled_coefs, local_weights)
        off_grid = summed.astype(jnp.bfloat16).astype(jnp.float32)
        angular_rows = rounded.reshape(hel_rows, rad_rows * vib_count, ang_count)
        grid = jnp.einsum(
            "kna,kag->kng", angular_rows, transform, preferred_element_type=jnp.float32
        )
        grid_values = (grid * potential_flat).astype(jnp.bfloat16)
        angular_part = jnp.einsum(
            "kng,kag->kna", grid_values, transform, preferred_element_type=jnp.float32
        )
        applied = SCALE_FACTOR * (off_grid + angular_part.reshape(hel_rows, rad_rows, flat_width))
        following = damp * (2.0 * applied - damp * previous)
        previous = current
        current = following
    shape = (hel_rows, rad_rows, vib_count, ang_count)
    return (previous.reshape(shape), current.reshape(shape))


def by_vibration(
    older_packet, newer_packet, kinetic, transform, potential, coupling, radial_weight, damping
):
    hel_rows, rad_rows, vib_count, ang_count = newer_packet.shape
    devices = lax.axis_size("rad")

    def scatter(array):
        return lax.all_to_all(array, "rad", split_axis=2, concat_axis=1, tiled=True)

    rounded = scatter(newer_packet.astype(jnp.bfloat16))
    previous = scatter(older_packet.astype(jnp.bfloat16)).astype(jnp.float32)
    pot = scatter(potential[None])[0].astype(jnp.float32)
    damp = lax.all_gather(damping, "rad", tiled=True)[None, :, None, None]
    weight = radial_weight[None, :, None, None]
    current = rounded.astype(jnp.float32)
    lower_coefs = from_behind(coupling, "hel", 1)
    coefs = jnp.concatenate([lower_coefs, coupling], axis=0).astype(jnp.float32)
    coefs = coefs[:, None, None, :]
    history = []
    for step in range(STEPS):
        lower = from_behind(rounded[-1:], "hel", 1)
        upper = from_behind(rounded[:1], "hel", -1)
        padded = jnp.concatenate([lower, rounded, upper], axis=0).astype(jnp.float32)
        mixed = coefs[:-1] * padded[:-2] + coefs[1:] * padded[2:]
        radial = jnp.einsum(
            "rs,ksva->krva", kinetic, rounded, preferred_element_type=jnp.float32
        )
        off_grid = radial + weight * mixed
        grid = jnp.einsum(
            "krva,kag->krvg", rounded, transform, preferred_element_type=jnp.float32
        )
        grid_values = (grid * pot[None]).astype(jnp.bfloat16)
        angular = jnp.einsum(
            "krvg,kag->krva", grid_values, transform, preferred_element_type=jnp.float32
        )
        applied = SCALE_FACTOR * (off_grid + angular)
        following = damp * (2.0 * applied - damp * previous)
        previous = current
        current = following
        rounded = current.astype(jnp.bfloat16)
        history.append(rounded)

    def gather(array):
        back = lax.all_to_all(array, "rad", split_axis=1, concat_axis=2, tiled=True)
        return back.astype(jnp.float32)

    return gather(history[-2]), gather(history[-1])


MESH = pl.DeviceIdType.MESH
POT, NEW, OLD, DAMP, OUT3, OUT4 = range(6)


def packet_kernel(
    n, hels,
    newer, older, kinetic, transform, potential, coupling, weight, damping,
    back3, back4,
    newer_v, older_v, kin, tr, pot_in, pot_wide, coef, coef_low, damp_own, damp_all, weight_all,
    damp_col, weight_col, send_pot, send_new, send_old, pot, x0, x1, x2, x3, x4, total, grid,
    low, high,
    in_sem, lane_sem, own_sem, rad_send, rad_recv, pot_send, pot_recv, hel_send, hel_recv, coef_sem,
):
    me = lax.axis_index("rad")
    hel = lax.axis_index("hel")
    rows = send_new.shape[1]
    ang = newer.shape[1]
    width = ang // hels
    has_low = hel > 0
    has_high = hel < hels - 1

    def shift(i):
        if n % 2:
            return i + 1
        return n // 2 + ((i + 1) // 2) * (1 - 2 * (i % 2))

    def target(i):
        return lax.rem(me + shift(i), n)

    def source(i):
        return lax.rem(me - shift(i) + n, n)

    def block(c):
        return pl.ds(pl.multiple_of(c * rows, rows), rows)

    loads = [
        pltpu.make_async_copy(src, dst, in_sem.at[s])
        for s, (src, dst) in enumerate(
            (
                (potential.at[:, :, pl.ds(pl.multiple_of(hel * width, width), width)], pot_in),
                (damping, damp_own),
                (coupling, coef),
                (weight, weight_all),
                (kinetic, kin),
                (transform, tr),
            )
        )
    ]

    def lanes(l):
        return pl.ds(pl.multiple_of(l * 128, 128), 128)

    def newer_load(l):
        return pltpu.make_async_copy(newer.at[:, lanes(l)], newer_v.at[l], lane_sem.at[0, l])

    def older_load(l):
        return pltpu.make_async_copy(older.at[:, lanes(l)], older_v.at[l], lane_sem.at[1, l])

    def each_lane(copy, method):
        @pl.loop(0, ang // 128)
        def _(l):
            getattr(copy(l), method)()

    for load in loads[:3]:
        load.start()
    each_lane(newer_load, "start")
    each_lane(older_load, "start")
    for load in loads[3:]:
        load.start()

    barrier = pltpu.get_barrier_semaphore()

    @pl.loop(1, n)
    def _(j):
        pl.semaphore_signal(
            barrier, inc=1, device_id={"rad": lax.rem(me + j, n)}, device_id_type=MESH
        )

    @pl.loop(1, hels)
    def _(j):
        pl.semaphore_signal(
            barrier, inc=1, device_id={"hel": lax.rem(hel + j, hels)}, device_id_type=MESH
        )

    pl.semaphore_wait(barrier, n + hels - 2)

    def over_rad(kind, src, dst, i):
        return pltpu.make_async_remote_copy(
            src_ref=src,
            dst_ref=dst,
            send_sem=rad_send.at[kind, i],
            recv_sem=rad_recv.at[kind, i],
            device_id={"rad": target(i)},
            device_id_type=MESH,
        )

    def pot_copy(i):
        return over_rad(POT, send_pot.at[i], pot.at[hel, block(me)], i)

    def new_copy(i):
        return over_rad(NEW, send_new.at[i], x1.at[block(me)], i)

    def old_copy(i):
        return over_rad(OLD, send_old.at[i], x0.at[block(me)], i)

    def damp_copy(i):
        return over_rad(DAMP, damp_own, damp_all.at[me], i)

    def out3_copy(i):
        return over_rad(OUT3, x3.at[block(target(i))], back3.at[me], i)

    def out4_copy(i):
        return over_rad(OUT4, x4.at[block(target(i))], back4.at[me], i)

    def pot_share(j):
        return pltpu.make_async_remote_copy(
            src_ref=pot.at[hel],
            dst_ref=pot.at[hel],
            send_sem=pot_send.at[j],
            recv_sem=pot_recv.at[j],
            device_id={"hel": lax.rem(hel + j, hels)},
            device_id_type=MESH,
        )

    coef_copy = pltpu.make_async_remote_copy(
        src_ref=coef,
        dst_ref=coef_low,
        send_sem=coef_sem.at[0],
        recv_sem=coef_sem.at[1],
        device_id={"hel": lax.rem(hel + 1, hels)},
        device_id_type=MESH,
    )

    def hel_up(step, x, c, sem):
        return pltpu.make_async_remote_copy(
            src_ref=x.at[c],
            dst_ref=low.at[step, c],
            send_sem=hel_send.at[step, 0, sem],
            recv_sem=hel_recv.at[step, 0, sem],
            device_id={"hel": lax.rem(hel + 1, hels)},
            device_id_type=MESH,
        )

    def hel_down(step, x, c, sem):
        return pltpu.make_async_remote_copy(
            src_ref=x.at[c],
            dst_ref=high.at[step, c],
            send_sem=hel_send.at[step, 1, sem],
            recv_sem=hel_recv.at[step, 1, sem],
            device_id={"hel": lax.rem(hel - 1 + hels, hels)},
            device_id_type=MESH,
        )

    def hel_start(step, x, c, sem):
        @pl.when(has_high)
        def _():
            hel_up(step, x, c, sem).start()

        @pl.when(has_low)
        def _():
            hel_down(step, x, c, sem).start()

    def hel_wait_recv(step, x, c, sem):
        @pl.when(has_low)
        def _():
            hel_up(step, x, c, sem).wait_recv()

        @pl.when(has_high)
        def _():
            hel_down(step, x, c, sem).wait_recv()

    def hel_wait_send(step, x, c, sem):
        @pl.when(has_high)
        def _():
            hel_up(step, x, c, sem).wait_send()

        @pl.when(has_low)
        def _():
            hel_down(step, x, c, sem).wait_send()

    def trailing(make, copy):
        @pl.loop(0, n - 1)
        def _(i):
            make(i)

            @pl.when(i > 0)
            def _():
                copy(i - 1).start()

    everything = pl.ds(0, n * rows)

    loads[0].wait()
    for l in range(width // 128):
        part = pot_in[:, :, 128 * l : 128 * (l + 1)].astype(jnp.float32)
        pot_wide[l] = part.reshape(pot_wide.shape[1:])

    def picked(ref, c):
        return jnp.concatenate(
            [
                ref[l, pl.ds(c, rows, stride=n), :]
                for l in range(ref.shape[0])
            ],
            axis=1,
        ).astype(jnp.bfloat16)

    def make_pot(i):
        send_pot[i] = picked(pot_wide, target(i))

    trailing(make_pot, pot_copy)
    pot[hel, block(me)] = picked(pot_wide, me)
    pot_copy(n - 2).start()

    each_lane(newer_load, "wait")

    def make_new(i):
        send_new[i] = picked(newer_v, target(i))

    trailing(make_new, new_copy)
    x1[block(me)] = picked(newer_v, me)
    new_copy(n - 2).start()

    loads[1].wait()
    loads[2].wait()

    @pl.loop(0, n - 1)
    def _(i):
        damp_copy(i).start()

    @pl.when(has_high)
    def _():
        coef_copy.start()

    each_lane(older_load, "wait")

    def make_old(i):
        send_old[i] = picked(older_v, target(i))

    trailing(make_old, old_copy)
    x0[block(me)] = picked(older_v, me)
    old_copy(n - 2).start()
    damp_all[me] = damp_own[...]

    @pl.when(jnp.logical_not(has_low))
    def _():
        low[...] = jnp.zeros_like(low)
        coef_low[...] = jnp.zeros_like(coef_low)

    @pl.when(jnp.logical_not(has_high))
    def _():
        high[...] = jnp.zeros_like(high)

    for load in loads[3:]:
        load.wait()

    @pl.loop(0, n - 1)
    def _(i):
        pot_copy(i).wait_recv()

    @pl.loop(1, hels)
    def _(j):
        pot_share(j).start()

    @pl.loop(0, n - 1)
    def _(i):
        damp_copy(i).wait_recv()

    @pl.when(has_low)
    def _():
        coef_copy.wait_recv()

    line = lax.broadcasted_iota(jnp.int32, (rows, rows), 0)
    lane = lax.broadcasted_iota(jnp.int32, (rows, rows), 1)

    def column(row):
        diagonal = jnp.where(line == lane, jnp.broadcast_to(row, (rows, rows)), 0.0)
        return jnp.broadcast_to(jnp.sum(diagonal, axis=1, keepdims=True), (rows, 128))

    @pl.loop(0, n)
    def _(c):
        damp_col[block(c)] = column(damp_all[c])

    for c in range(n):
        part = weight_all[:, c * rows : (c + 1) * rows]
        weight_col[c * rows : (c + 1) * rows] = column(part)

    hel_start(0, x1, block(me), 0)

    @pl.loop(0, n - 1)
    def _(i):
        new_copy(i).wait_recv()
        hel_start(0, x1, block(source(i)), n - shift(i))

    @pl.loop(1, hels)
    def _(j):
        pot_share(j).wait_recv()

    def to_grid(x, span):
        values = jnp.dot(x[span], tr[...], preferred_element_type=jnp.float32)
        for t in range(hels):
            part = values[:, t * width : (t + 1) * width] * pot[t, span].astype(jnp.float32)
            grid[span, t * width : (t + 1) * width] = part.astype(jnp.bfloat16)

    def from_grid(span):
        return lax.dot_general(
            grid[span], tr[...], (((1,), (1,)), ((), ())), preferred_element_type=jnp.float32
        )

    def radial(x):
        return jnp.dot(kin[...], x[...], preferred_element_type=jnp.float32)

    def multiply(x):
        to_grid(x, everything)
        total[...] = from_grid(everything) + radial(x)

    lower_coef = coef_low[...].astype(jnp.float32)
    upper_coef = coef[...].astype(jnp.float32)

    def finish(step, prev, c):
        span = block(c)
        damp = damp_col[span, 0:1]
        mixed = lower_coef * low[step, span].astype(jnp.float32)
        mixed = mixed + upper_coef * high[step, span].astype(jnp.float32)
        applied = SCALE_FACTOR * (total[span] + weight_col[span, 0:1] * mixed)
        following = damp * (2.0 * applied - damp * prev[span].astype(jnp.float32))
        return following.astype(jnp.bfloat16)

    multiply(x1)

    def hel_arrived(step, x):
        @pl.loop(0, n)
        def _(i):
            hel_wait_recv(step, x, block(lax.rem(me + i, n)), i)

    hel_arrived(0, x1)

    def next_block(c, sem):
        x2[block(c)] = finish(0, x0, c)
        hel_start(1, x2, block(c), sem)

    next_block(me, 0)

    @pl.loop(0, n - 1)
    def _(i):
        old_copy(i).wait_recv()
        next_block(source(i), n - shift(i))

    multiply(x2)
    hel_arrived(1, x2)

    def make_out3(i):
        x3[block(target(i))] = finish(1, x1, target(i))

    trailing(make_out3, out3_copy)
    x3[block(me)] = finish(1, x1, me)
    out3_copy(n - 2).start()
    hel_start(2, x3, everything, 0)

    multiply(x3)
    hel_wait_recv(2, x3, everything, 0)

    def make_out4(i):
        x4[block(target(i))] = finish(2, x2, target(i))

    trailing(make_out4, out4_copy)
    x4[block(me)] = finish(2, x2, me)
    out4_copy(n - 2).start()

    own = [
        pltpu.make_async_copy(x.at[block(me)], back.at[me], own_sem.at[j])
        for j, (x, back) in enumerate(((x3, back3), (x4, back4)))
    ]
    for copy in own:
        copy.start()

    @pl.loop(0, n - 1)
    def _(i):
        out3_copy(i).wait_recv()
        out4_copy(i).wait_recv()

    @pl.loop(0, n - 1)
    def _(i):
        for copy in (pot_copy, new_copy, old_copy, damp_copy, out3_copy, out4_copy):
            copy(i).wait_send()

    @pl.loop(1, hels)
    def _(j):
        pot_share(j).wait_send()

    @pl.when(has_high)
    def _():
        coef_copy.wait_send()

    hel_wait_send(2, x3, everything, 0)

    @pl.loop(0, n)
    def _(i):
        hel_wait_send(0, x1, block(lax.rem(me + i, n)), i)
        hel_wait_send(1, x2, block(lax.rem(me + i, n)), i)

    for copy in own:
        copy.wait()


def place_kernel(n, back3, back4, out_old, out_new, held, wide, in_sem, out_sem):
    rows, ang = back3.shape[1:]
    groups = ang // 128
    pairs = ((back3, out_old), (back4, out_new))

    def load(s, l):
        return pltpu.make_async_copy(
            pairs[s][0].at[:, :, pl.ds(128 * l, 128)], held.at[s, l], in_sem.at[s, l]
        )

    def unload(s, l):
        return pltpu.make_async_copy(
            wide.at[s, l], pairs[s][1].at[:, pl.ds(128 * l, 128)], out_sem.at[s, l]
        )

    every = [(s, l) for s in range(2) for l in range(groups)]
    for s, l in every:
        load(s, l).start()
    for s, l in every:
        load(s, l).wait()
        for c in range(n):
            wide[s, l, pl.ds(c, rows, stride=n), :] = held[s, l, c].astype(jnp.float32)
        unload(s, l).start()
    for s, l in every:
        unload(s, l).wait()


def one_vibration(
    older_packet, newer_packet, kinetic, transform, potential, coupling, radial_weight, damping
):
    _, rows, n, ang = newer_packet.shape
    hels = lax.axis_size("hel")
    width = ang // hels
    points = n * rows
    bf16, f32 = jnp.bfloat16, jnp.float32
    vector = pltpu.VMEM((points, ang), bf16)
    blocks = pltpu.VMEM((n, rows, ang), bf16)
    wide = pltpu.VMEM((points, ang), f32)
    flat = jax.ShapeDtypeStruct((points, ang), f32)
    back = jax.ShapeDtypeStruct((n, rows, ang), bf16)
    anywhere = pl.BlockSpec(memory_space=pl.ANY)
    sem = pltpu.SemaphoreType.DMA
    groups = ang // 128
    backs = pl.pallas_call(
        functools.partial(packet_kernel, n, hels),
        out_shape=(back, back),
        in_specs=[anywhere] * 8,
        out_specs=(anywhere, anywhere),
        scratch_shapes=[
            pltpu.VMEM((ang // 128, points, 128), f32),
            pltpu.VMEM((ang // 128, points, 128), f32),
            pltpu.VMEM((points, points), bf16),
            pltpu.VMEM((ang, ang), bf16),
            pltpu.VMEM((rows, n, width), bf16),
            pltpu.VMEM((width // 128, points, 128), f32),
            pltpu.VMEM((1, ang), bf16),
            pltpu.VMEM((1, ang), bf16),
            pltpu.VMEM((1, rows), f32),
            pltpu.VMEM((n, 1, rows), f32),
            pltpu.VMEM((1, points), f32),
            pltpu.VMEM((points, 128), f32),
            pltpu.VMEM((points, 128), f32),
            pltpu.VMEM((n, rows, width), bf16),
            blocks,
            blocks,
            pltpu.VMEM((hels, points, width), bf16),
            vector,
            vector,
            vector,
            vector,
            vector,
            wide,
            vector,
            pltpu.VMEM((STEPS, points, ang), bf16),
            pltpu.VMEM((STEPS, points, ang), bf16),
            sem((6,)),
            sem((2, groups)),
            sem((2,)),
            sem((6, n)),
            sem((6, n)),
            sem((hels,)),
            sem((hels,)),
            sem((STEPS, 2, n)),
            sem((STEPS, 2, n)),
            sem((2,)),
        ],
        compiler_params=pltpu.CompilerParams(
            collective_id=0, has_side_effects=True, vmem_limit_bytes=60 * 1024 * 1024
        ),
    )(
        newer_packet.reshape(points, ang),
        older_packet.reshape(points, ang),
        kinetic,
        transform[0],
        potential,
        coupling,
        radial_weight.reshape(1, points),
        damping.reshape(1, rows),
    )
    outs = pl.pallas_call(
        functools.partial(place_kernel, n),
        out_shape=(flat, flat),
        in_specs=[anywhere] * 2,
        out_specs=(anywhere, anywhere),
        scratch_shapes=[
            pltpu.VMEM((2, groups, n, rows, 128), bf16),
            pltpu.VMEM((2, groups, points, 128), f32),
            sem((2, groups)),
            sem((2, groups)),
        ],
    )(*backs)
    shape = newer_packet.shape
    return outs[0].reshape(shape), outs[1].reshape(shape)


def fits(packet):
    hel_rows, rows, vibs, ang = packet.shape
    hels = lax.axis_size("hel")
    return (
        STEPS == 3
        and hel_rows == 1
        and vibs == lax.axis_size("rad")
        and vibs > 1
        and hels > 1
        and rows % 16 == 0
        and ang % (hels * 128) == 0
        and rows * vibs <= 512
        and ang <= 1024
    )


def whole_body(older_packet, newer_packet, *rest):
    if fits(newer_packet):
        return one_vibration(older_packet, newer_packet, *rest)
    if newer_packet.shape[2] % lax.axis_size("rad") == 0:
        return by_vibration(older_packet, newer_packet, *rest)
    return body(older_packet, newer_packet, *rest)


def solution(mesh):
    return jax.shard_map(
        whole_body,
        mesh=mesh,
        in_specs=(
            P("hel", "rad", None, None),
            P("hel", "rad", None, None),
            P(),
            P("hel", None, None),
            P("rad", None, None),
            P("hel", None),
            P(),
            P("rad"),
        ),
        out_specs=(P("hel", "rad", None, None), P("hel", "rad", None, None)),
        check_vma=False,
    )
```
